32 devices in a mesh: view: 16 (over z, y, x), head: 2 (over core).
Axes of the slice: x: 2, y: 2, z: 4, core: 2. Of those that a mesh axis runs over, the one named last changes fastest.
Arguments:
- query_tokens: bfloat16 [4096, 1024], P('view'), may hold values from -360 to 360
- image_tokens: bfloat16 [16384, 1024], P('view'), may hold values from -6 to 6
- w_query: bfloat16 [1024, 1024], P(None, 'head'), may hold values from -0.1875 to 0.1875
- w_key: bfloat16 [1024, 1024], P(None, 'head'), may hold values from -0.1875 to 0.1875
- w_value: bfloat16 [1024, 1024], P(None, 'head'), may hold values from -0.1875 to 0.1875
- w_out: bfloat16 [1024, 1024], P('head'), may hold values from -0.1875 to 0.1875
- vis_list: int32 [32, 12], P('view'), may hold values from 0 to 127, as said below
- vis_count: int32 [32], P('view'), may hold values from 8 to 12
Outputs:
- attended: bfloat16 [4096, 1024], P('view', 'head')
The draws below stay inside these ranges and needn't reach their ends.
Inputs may be any that keep to these rules, and one draw needn't show every extreme that they name: `vis_list`: entry j of row b names a global image block (block g holds image tokens g * 128 onward); the first vis_count[b] entries are the visible ones, the rest padding. All entries of one row lie on different devices of view. Among all entries of the 2 rows held by one device, those lying on one source device name the same block.
All inputs are finite; a program needn't handle non-finite values.
Results may differ from the reference program's by a relative error of at most 0.0085.
The reference program's roundings to bfloat16 on the way (of `queries`, `probs` and `context`) count: a program that leaves them out, or rounds other values in their place, can miss the bound.
Values may be sent and summed in bfloat16 or wider, within the bound.
A program may use at most 64 MiB of HBM per device.

```python
import math
import jax
import jax.numpy as jnp
from jax import lax

D = 1024
HEADS = 8
HEAD_DIM = 128
BLOCK = 128
QB_DEV = 2
BLK_DEV = 8
MAXVIS = 12
TRI = 4096
IMG = 16384
QBLK = 32


def visibility(key):
    base = jax.random.fold_in(key, 11)
    pick_key, order_key, count_key, full_key = jax.random.split(base, 4)
    device_count = QBLK // QB_DEV
    chosen_block = jax.random.randint(pick_key, (device_count, device_count), 0, BLK_DEV)
    ranking = jax.random.randint(order_key, (QBLK, device_count), 0, 1 << 16) * device_count + jnp.arange(device_count)[None, :]
    sources = jnp.argsort(ranking, axis=1)[:, :MAXVIS].astype(jnp.int32)
    owner = jnp.arange(QBLK) // QB_DEV
    blocks = jnp.take_along_axis(chosen_block[owner], sources, axis=1)
    block_ids = (sources * BLK_DEV + blocks).astype(jnp.int32)
    counts = jax.random.randint(count_key, (QBLK,), device_count // 2, MAXVIS + 1)
    fullest = jax.random.randint(full_key, (), 0, QBLK)
    counts = jnp.where(jnp.arange(QBLK) == fullest, MAXVIS, counts).astype(jnp.int32)
    return (block_ids, counts)


def draw_vis_list(key, part):
    return visibility(key)[0]


def draw_vis_count(key, part):
    return visibility(key)[1]


def draw_query_tokens(key, part):
    base_key = jax.random.fold_in(jax.random.fold_in(key, 3), 0)
    values = jax.random.truncated_normal(base_key, -6.0, 6.0, (TRI, D), jnp.float32)
    return values.astype(jnp.bfloat16)


def steps_of(own_key, dims, cuts, smallest, top_value):
    def one(position, shards_of):
        heights = jax.random.uniform(jax.random.fold_in(jax.random.fold_in(own_key, 6), position), (shards_of,), jnp.float32, smallest / len(cuts), top_value / len(cuts))
        return jnp.repeat(jnp.exp(heights), dims[position] // shards_of).reshape((-1,) + (1,) * (len(dims) - position - 1))

    loudness = one(*cuts[0])
    for cut in cuts[1:]:
        loudness = loudness * one(*cut)
    return loudness


def normal_values(own_key, shape, deviation, limit, shards=(), held_as=jnp.bfloat16):
    values = jax.random.normal(own_key, shape, jnp.float32) * deviation
    if len(shards) > 0:
        values = steps_of(own_key, shape, shards, -0.22, 0.18) * values
    return jnp.clip(values, min=-limit, max=limit).astype(held_as)


def setup_inputs(seed: int = 0) -> dict:
    streams_of = jax.random.split(jax.random.key(seed), 9)
    return {
        "query_tokens": draw_query_tokens(jax.random.fold_in(streams_of[8], 71), 0),
        "image_tokens": normal_values(streams_of[1], (IMG, D), 1.0, 6.0, ((0, 16),)),
        "w_query": normal_values(streams_of[2], (D, D), D ** -0.5, 0.1875, ((1, 2),)),
        "w_key": normal_values(streams_of[3], (D, D), D ** -0.5, 0.1875, ((1, 2),)),
        "w_value": normal_values(streams_of[4], (D, D), D ** -0.5, 0.1875, ((1, 2),)),
        "w_out": normal_values(streams_of[5], (D, D), D ** -0.5, 0.1875, ((0, 2),)),
        "vis_list": draw_vis_list(jax.random.fold_in(streams_of[8], 71), 0),
        "vis_count": draw_vis_count(jax.random.fold_in(streams_of[8], 71), 0),
    }


def reference(query_tokens, image_tokens, w_query, w_key, w_value, w_out, vis_list, vis_count):
    queries = jnp.dot(query_tokens, w_query, preferred_element_type=jnp.float32).astype(jnp.bfloat16)
    image_keys = jnp.dot(image_tokens, w_key, preferred_element_type=jnp.float32).astype(jnp.bfloat16)
    image_values = jnp.dot(image_tokens, w_value, preferred_element_type=jnp.float32).astype(jnp.bfloat16)
    key_blocks = image_keys.reshape(-1, BLOCK, D)
    value_blocks = image_values.reshape(-1, BLOCK, D)
    query_heads = queries.reshape(-1, BLOCK, HEADS, HEAD_DIM)
    positions = jnp.arange(MAXVIS * BLOCK, dtype=jnp.int32) // BLOCK

    def attend_block(inputs):
        query_rows, block_ids, visible_count = inputs
        block_keys = jnp.take(key_blocks, block_ids.astype(jnp.int32), axis=0).reshape(MAXVIS * BLOCK, HEADS, HEAD_DIM).astype(jnp.float32)
        block_values = jnp.take(value_blocks, block_ids.astype(jnp.int32), axis=0).reshape(MAXVIS * BLOCK, HEADS, HEAD_DIM).astype(jnp.float32)
        scores = jnp.einsum('ihd,khd->hik', query_rows.astype(jnp.float32), block_keys) * (1.0 / math.sqrt(HEAD_DIM))
        allowed = (positions < visible_count)[None, None, :]
        peak = lax.optimization_barrier(jnp.max(jnp.where(allowed, scores, -1e+30), axis=2, keepdims=True))
        raised = jnp.where(allowed, jnp.exp(scores - peak), 0.0)
        probs = (raised / lax.optimization_barrier(jnp.sum(raised, axis=2, keepdims=True))).astype(jnp.bfloat16)
        probs = lax.optimization_barrier(probs)
        context = jnp.einsum('hik,khd->ihd', probs.astype(jnp.float32), block_values)
        return context.astype(jnp.bfloat16).reshape(BLOCK, D)
    context = lax.map(attend_block, (query_heads, vis_list, vis_count)).reshape(-1, D)
    return jnp.dot(context, w_out, preferred_element_type=jnp.float32).astype(jnp.bfloat16)
```

```python
import functools
import math

import jax
import jax.numpy as jnp
from jax import lax
from jax.experimental import pallas as pl
from jax.experimental.pallas import tpu as pltpu
from jax.sharding import PartitionSpec as P

HEAD_DIM = 128
BLOCK = 128
LINE = 4
MESH = pl.DeviceIdType.MESH
HIDDEN = -1e30
NT = (((1,), (1,)), ((), ()))


def flipped(index, offset, view_count):
    result, bit = 0, 1
    while bit < view_count:
        flip = (index // bit + offset // bit) % 2
        result = result + flip * bit
        bit *= 2
    return result


def kernel(
    n,
    heads,
    list_ref,
    count_ref,
    x_hbm,
    qt_hbm,
    wq_hbm,
    wk_hbm,
    wv_hbm,
    wo_hbm,
    out_ref,
    x_vm,
    qt_vm,
    wq_vm,
    wk_vm,
    wv_vm,
    wvt_vm,
    wo_all,
    ask_vm,
    asked_vm,
    asked_sm,
    picked,
    arrived,
    q_vm,
    k_vm,
    vt_vm,
    acc_vm,
    stat_vm,
    part_out,
    part_in,
    stat_in,
    ctx_all,
    load_sem,
    ask_send,
    ask_recv,
    own_sem,
    tok_send,
    tok_recv,
    fwd_send,
    fwd_recv,
    wo_send,
    wo_recv,
    q_send,
    q_recv,
    part_send,
    part_recv,
    stat_send,
    stat_recv,
    ctx_send,
    ctx_recv,
):
    me = lax.axis_index("view")
    core = lax.axis_index("head")
    rows, width = out_ref.shape
    panel = wq_vm.shape[1]
    head_count = panel // HEAD_DIM
    depth = x_vm.shape[-1]
    block_count = x_vm.shape[0]
    plane = n // LINE
    query_blocks = rows // BLOCK
    factor = math.log2(math.e) / math.sqrt(HEAD_DIM)

    level = me // plane
    inner = (level + level // 2) % 2
    def reach(step):
        return LINE - 1 - step + inner * (1 - step // 2) * (2 * (step % 2) - 1)

    def peer(offset):
        return (flipped(me, offset, n), core)

    def along(offset):
        return peer(offset * plane)

    def sibling(step):
        return (core + step) % heads

    def before(step):
        return (core + heads - step) % heads

    def remote(source, target, send, recv, device):
        return pltpu.make_async_remote_copy(
            src_ref=source,
            dst_ref=target,
            send_sem=send,
            recv_sem=recv,
            device_id=device,
            device_id_type=MESH,
        )

    barrier = pltpu.get_barrier_semaphore()
    for slot in range(1, n):
        pl.semaphore_signal(barrier, inc=1, device_id=peer(slot), device_id_type=MESH)
    for step in range(1, heads):
        pl.semaphore_signal(
            barrier, inc=1, device_id=(me, sibling(step)), device_id_type=MESH
        )

    loads = [
        pltpu.make_async_copy(source, target, load_sem.at[position])
        for position, (source, target) in enumerate(
            [
                (x_hbm, x_vm),
                (qt_hbm, qt_vm),
                (wq_hbm, wq_vm),
                (wk_hbm, wk_vm),
                (wv_hbm, wv_vm),
                (
                    wo_hbm.at[:, pl.ds(pl.multiple_of(core * width, 128), width)],
                    wo_all.at[core],
                ),
            ]
        )
    ]
    for position in (1, 2, 0, 4, 3, 5):
        loads[position].start()

    line_shape = (1, ask_vm.shape[1])
    first = lax.broadcasted_iota(jnp.int32, line_shape, 1) * block_count
    number = jnp.zeros(line_shape, jnp.int32)
    flags = [jnp.ones(line_shape, jnp.int32) for _ in range(query_blocks)]
    for block in range(query_blocks):
        count = count_ref[block]
        for entry in range(list_ref.shape[1]):
            distance = list_ref[block, entry] - first
            hit = jnp.logical_and(distance >= 0, distance < block_count)
            unseen = jnp.where(entry < count, 0, 1)
            number = jnp.where(hit, distance, number)
            flags[block] = jnp.minimum(flags[block], jnp.where(hit, unseen, 1))
    ask_vm[0:1] = number
    for block in range(query_blocks):
        ask_vm[block + 1 : block + 2] = flags[block]

    def ask(slot):
        return remote(
            ask_vm, asked_vm.at[slot], ask_send.at[slot], ask_recv.at[slot], peer(slot)
        )

    pl.semaphore_wait(barrier, n - 1 + heads - 1)
    for slot in range(1, n):
        ask(slot).start()

    def token(step, place):
        return remote(
            picked.at[step, place],
            arrived.at[step, place, core],
            tok_send.at[step, place],
            tok_recv.at[step, place],
            peer(place),
        )

    def forward(step, place, hop, part):
        return remote(
            arrived.at[step, place, part],
            arrived.at[step, place, part],
            fwd_send.at[step, place, hop],
            fwd_recv.at[step, place, hop],
            (me, sibling(hop)),
        )

    def weight(hop, part, columns):
        return remote(
            wo_hbm.at[:, pl.ds(pl.multiple_of(columns * width, 128), width)],
            wo_all.at[part],
            wo_send.at[hop],
            wo_recv.at[hop],
            (me, sibling(hop)),
        )

    def context(hop, head, part):
        lanes = pl.ds(head * HEAD_DIM, HEAD_DIM)
        return remote(
            ctx_all.at[part, :, lanes],
            ctx_all.at[part, :, lanes],
            ctx_send.at[hop, head],
            ctx_recv.at[hop, head],
            (me, sibling(hop)),
        )

    routes = [(0, 1, 1), (0, 3, 3), (1, 3, 2), (2, 1, 3), (3, 1, 2)]

    def query(route, head):
        here, to, there = routes[route]
        return remote(
            q_vm.at[here, head],
            q_vm.at[there, head],
            q_send.at[route, head],
            q_recv.at[there, head],
            along(to),
        )

    def query_arrived(slot, head):
        return remote(
            q_vm.at[0, head],
            q_vm.at[slot, head],
            q_send.at[0, head],
            q_recv.at[slot, head],
            along(1),
        )

    def partial(step, slot, to):
        return [
            remote(
                part_out.at[step],
                part_in.at[slot],
                part_send.at[step],
                part_recv.at[slot],
                along(to),
            ),
            remote(
                stat_vm.at[step],
                stat_in.at[slot],
                stat_send.at[step],
                stat_recv.at[slot],
                along(to),
            ),
        ]

    def send(step, slot, to):
        part_out[step] = acc_vm[step].astype(part_out.dtype)
        for copy in partial(step, slot, to):
            copy.start()

    def merge(step, slot):
        for copy in partial(0, slot, 1):
            copy.wait_recv()
        for head in range(head_count):
            lanes = pl.ds(head * HEAD_DIM, HEAD_DIM)
            peak = stat_vm[step, pl.ds(head, 1)]
            other = stat_in[slot, pl.ds(head, 1)]
            top = jnp.maximum(peak, other)
            mine = jnp.exp2(peak - top)
            theirs = jnp.exp2(other - top)
            total = pl.ds(head_count + head, 1)
            stat_vm[step, pl.ds(head, 1)] = top
            stat_vm[step, total] = (
                stat_vm[step, total] * mine + stat_in[slot, total] * theirs
            )
            acc_vm[step, lanes] = acc_vm[step, lanes] * mine + (
                part_in[slot, lanes].astype(jnp.float32) * theirs
            )

    loads[1].wait()
    loads[2].wait()
    for head in range(head_count):
        lanes = pl.ds(head * HEAD_DIM, HEAD_DIM)
        q_vm[0, head] = jnp.dot(
            qt_vm[...], wq_vm[:, lanes], preferred_element_type=jnp.float32
        ).astype(q_vm.dtype)

    @pl.when(inner == 0)
    def _():
        for head in range(head_count):
            query(0, head).start()

    loads[0].wait()
    for slot in range(1, n):
        ask(slot).wait_recv()
    asked_vm[0] = ask_vm[...]
    fetch = pltpu.make_async_copy(asked_vm, asked_sm, own_sem.at[0])
    fetch.start()
    fetch.wait()

    def asked(step, place, row, source):
        return asked_sm[reach(step) * plane + place, row, source]

    for step in range(LINE):
        for place in range(1, plane):
            picked[step, place] = x_vm[asked(step, place, 0, me), core]
            token(step, place).start()
    for hop in range(1, heads):
        weight(hop, core, sibling(hop)).start()
    for step in range(LINE):
        arrived[step, 0] = x_vm[asked(step, 0, 0, me)]
    loads[4].wait()
    wvt_vm[...] = wv_vm[...].T
    loads[3].wait()

    @pl.when(inner == 1)
    def _():
        for head in range(head_count):
            query_arrived(1, head).wait_recv()
            query(2, head).start()
        for head in range(head_count):
            query(1, head).start()
        for head in range(head_count):
            query_arrived(2, head).wait_recv()
            query(3, head).start()

    half = plane // 2

    def take_in(step, places):
        for place in places:
            if place:
                token(step, place).wait_recv()
                for hop in range(1, heads):
                    forward(step, place, hop, core).start()
        for place in places:
            if place:
                for hop in range(1, heads):
                    forward(step, place, hop, before(hop)).wait_recv()

    def project(step, start):
        tokens = arrived[step, pl.ds(start, half)].reshape(half * BLOCK, depth)
        span = pl.ds(start * BLOCK, half * BLOCK)
        k_vm[span] = jnp.dot(
            tokens, wk_vm[...], preferred_element_type=jnp.float32
        ).astype(k_vm.dtype)
        vt_vm[:, span] = lax.dot_general(
            wvt_vm[...], tokens, NT, preferred_element_type=jnp.float32
        ).astype(vt_vm.dtype)

    def attend(step):
        lane_block = lax.broadcasted_iota(jnp.int32, (1, rows), 1) // BLOCK
        masks = []
        for place in range(plane):
            unseen = jnp.zeros((1, rows), jnp.int32)
            for block in range(query_blocks):
                flag = asked(step, 0, block + 1, flipped(me, place, n))
                unseen = jnp.where(lane_block == block, flag, unseen)
            masks.append(unseen.astype(jnp.float32) * HIDDEN)
        for head in range(head_count):
            lanes = pl.ds(head * HEAD_DIM, HEAD_DIM)
            scores = lax.dot_general(
                k_vm[:, lanes],
                q_vm[reach(step), head],
                NT,
                preferred_element_type=jnp.float32,
            )
            scores = [
                scores[place * BLOCK : (place + 1) * BLOCK] + masks[place]
                for place in range(plane)
            ]
            peak = functools.reduce(jnp.maximum, scores)
            peak = jnp.max(peak, axis=0, keepdims=True) * factor
            raised = [jnp.exp2(part * factor - peak) for part in scores]
            total = functools.reduce(jnp.add, raised)
            stat_vm[step, pl.ds(head, 1)] = peak
            stat_vm[step, pl.ds(head_count + head, 1)] = jnp.sum(
                total, axis=0, keepdims=True
            )
            probs = jnp.concatenate([part.astype(vt_vm.dtype) for part in raised], axis=0)
            acc_vm[step, lanes] = jnp.dot(
                vt_vm[lanes], probs, preferred_element_type=jnp.float32
            )

    def one_step(step, carry):
        take_in(step, range(half))
        project(step, 0)
        take_in(step, range(half, plane))
        project(step, half)

        @pl.when(jnp.logical_and(inner == 0, step < LINE - 1))
        def _():
            for head in range(head_count):
                query_arrived(LINE - 1 - step, head).wait_recv()

        attend(step)

        @pl.when(jnp.logical_and(inner == 0, step < LINE - 1))
        def _():
            send(step, step, 1)

        @pl.when(jnp.logical_and(inner == 1, step == 0))
        def _():
            for head in range(head_count):
                query_arrived(3, head).wait_recv()
                query(4, head).start()
            for head in range(head_count):
                query(0, head).start()

        @pl.when(jnp.logical_and(inner == 1, jnp.logical_and(step > 0, step < LINE - 1)))
        def _():
            merge(step - 1, step - 1)
            send(step - 1, step + 2, 3)

        @pl.when(jnp.logical_and(inner == 1, step == LINE - 2))
        def _():
            merge(LINE - 2, 3)
            send(LINE - 2, 2, 1)

        return carry

    lax.fori_loop(0, LINE, one_step, 0)
    last = LINE - 1

    @pl.when(inner == 1)
    def _():
        merge(last, 4)

    merge(last, 2)
    for head in range(head_count):
        lanes = pl.ds(head * HEAD_DIM, HEAD_DIM)
        merged = acc_vm[last, lanes] / stat_vm[last, pl.ds(head_count + head, 1)]
        ctx_all[core, :, lanes] = merged.T.astype(ctx_all.dtype)
        for hop in range(1, heads):
            context(hop, head, core).start()
    loads[5].wait()
    result = jnp.dot(ctx_all[core], wo_all[core], preferred_element_type=jnp.float32)
    for hop in range(1, heads):
        part = before(hop)
        weight(hop, part, core).wait_recv()
        for head in range(head_count):
            context(hop, head, part).wait_recv()
        result = result + jnp.dot(
            ctx_all[part], wo_all[part], preferred_element_type=jnp.float32
        )
    out_ref[...] = result.astype(out_ref.dtype)

    for slot in range(1, n):
        ask(slot).wait_send()
    for step in range(LINE):
        for place in range(1, plane):
            token(step, place).wait_send()
            for hop in range(1, heads):
                forward(step, place, hop, core).wait_send()
    for head in range(head_count):
        query(0, head).wait_send()

    @pl.when(inner == 1)
    def _():
        for route in range(1, len(routes)):
            for head in range(head_count):
                query(route, head).wait_send()

    for step in range(LINE - 1):
        for copy in partial(step, 0, 1):
            copy.wait_send()
    for hop in range(1, heads):
        weight(hop, core, sibling(hop)).wait_send()
        for head in range(head_count):
            context(hop, head, core).wait_send()


def per_device(query_tokens, image_tokens, w_query, w_key, w_value, w_out, vis_list, vis_count):
    n = lax.axis_size("view")
    heads = lax.axis_size("head")
    rows, depth = query_tokens.shape
    panel = w_query.shape[1]
    head_count = panel // HEAD_DIM
    width = w_out.shape[1] // heads
    block_count = image_tokens.shape[0] // BLOCK
    part_rows = BLOCK // heads
    query_blocks = vis_list.shape[0]
    plane = n // LINE
    lanes = -(-n // 128) * 128

    anywhere = pl.BlockSpec(memory_space=pltpu.HBM)
    vmem = pl.BlockSpec(memory_space=pltpu.VMEM)
    smem = pl.BlockSpec(memory_space=pltpu.SMEM)
    dtype = image_tokens.dtype
    dma = pltpu.SemaphoreType.DMA
    return pl.pallas_call(
        functools.partial(kernel, n, heads),
        out_shape=jax.ShapeDtypeStruct((rows, width), dtype),
        in_specs=[smem] * 2 + [anywhere] * 6,
        out_specs=vmem,
        scratch_shapes=[
            pltpu.VMEM((block_count, heads, part_rows, depth), dtype),
            pltpu.VMEM((rows, depth), dtype),
            pltpu.VMEM((depth, panel), dtype),
            pltpu.VMEM((depth, panel), dtype),
            pltpu.VMEM((depth, panel), dtype),
            pltpu.VMEM((panel, depth), dtype),
            pltpu.VMEM((heads, panel, width), dtype),
            pltpu.VMEM((1 + query_blocks, lanes), jnp.int32),
            pltpu.VMEM((n, 1 + query_blocks, lanes), jnp.int32),
            pltpu.SMEM((n, 1 + query_blocks, lanes), jnp.int32),
            pltpu.VMEM((LINE, plane, part_rows, depth), dtype),
            pltpu.VMEM((LINE, plane, heads, part_rows, depth), dtype),
            pltpu.VMEM((LINE, head_count, rows, HEAD_DIM), dtype),
            pltpu.VMEM((plane * BLOCK, panel), dtype),
            pltpu.VMEM((panel, plane * BLOCK), dtype),
            pltpu.VMEM((LINE, panel, rows), jnp.float32),
            pltpu.VMEM((LINE, 2 * head_count, rows), jnp.float32),
            pltpu.VMEM((LINE - 1, panel, rows), dtype),
            pltpu.VMEM((5, panel, rows), dtype),
            pltpu.VMEM((5, 2 * head_count, rows), jnp.float32),
            pltpu.VMEM((heads, rows, panel), dtype),
            dma((6,)),
            dma((n,)),
            dma((n,)),
            dma((1,)),
            dma((LINE, plane)),
            dma((LINE, plane)),
            dma((LINE, plane, heads)),
            dma((LINE, plane, heads)),
            dma((heads,)),
            dma((heads,)),
            dma((5, head_count)),
            dma((LINE, head_count)),
            dma((LINE - 1,)),
            dma((5,)),
            dma((LINE - 1,)),
            dma((5,)),
            dma((heads, head_count)),
            dma((heads, head_count)),
        ],
        compiler_params=pltpu.CompilerParams(
            collective_id=0, has_side_effects=True, vmem_limit_bytes=int(53.6 * 2**20)
        ),
    )(
        vis_list,
        vis_count,
        image_tokens.reshape(block_count, heads, part_rows, depth),
        query_tokens,
        w_query,
        w_key,
        w_value,
        w_out,
    )


def solution(mesh):
    return jax.shard_map(
        per_device,
        mesh=mesh,
        in_specs=(
            P("view", None),
            P("view", None),
            P(None, "head"),
            P(None, "head"),
            P(None, "head"),
            P("head", None),
            P("view", None),
            P("view"),
        ),
        out_specs=P("view", "head"),
        check_vma=False,
    )
```

```python
import functools
import math

import jax
import jax.numpy as jnp
from jax import lax
from jax.experimental import pallas as pl
from jax.experimental.pallas import tpu as pltpu
from jax.sharding import PartitionSpec as P

HEAD_DIM = 128
BLOCK = 128
LINE = 4
MESH = pl.DeviceIdType.MESH
HIDDEN = -1e30
NT = (((1,), (1,)), ((), ()))


def flipper(index, count):
    changes, bit = [], 1
    while bit < count:
        changes.append((bit, bit - 2 * bit * lax.rem(lax.div(index, bit), 2)))
        bit *= 2

    def flipped(offset):
        result = index
        for bit, change in changes:
            if offset // bit % 2:
                result = result + change
        return result

    return flipped


def kernel(
    n,
    heads,
    list_hbm,
    count_hbm,
    x_hbm,
    qt_hbm,
    wq_hbm,
    wk_hbm,
    wv_hbm,
    wo_hbm,
    out_ref,
    list_ref,
    count_ref,
    x_vm,
    qt_vm,
    wq_vm,
    wk_vm,
    wv_vm,
    wvt_vm,
    wo_all,
    ask_vm,
    asked_vm,
    asked_sm,
    picked,
    arrived,
    q_vm,
    k_vm,
    vt_vm,
    acc_vm,
    stat_vm,
    part_out,
    part_in,
    stat_in,
    ctx_all,
    list_sem,
    load_sem,
    ask_send,
    ask_recv,
    own_sem,
    tok_send,
    tok_recv,
    fwd_send,
    fwd_recv,
    wo_send,
    wo_recv,
    q_send,
    q_recv,
    part_send,
    part_recv,
    stat_send,
    stat_recv,
    ctx_send,
    ctx_recv,
):
    me = lax.axis_index("view")
    core = lax.axis_index("head")
    rows, width = out_ref.shape
    panel = wq_vm.shape[1]
    head_count = panel // HEAD_DIM
    depth = x_vm.shape[-1]
    block_count = x_vm.shape[0]
    plane = n // LINE
    query_blocks = rows // BLOCK
    factor = math.log2(math.e) / math.sqrt(HEAD_DIM)

    level = lax.div(me, plane)
    inner = lax.rem(level + lax.div(level, 2), 2)
    flipped = flipper(me, n)

    def half_of(step):
        return step // 2 if isinstance(step, int) else lax.div(step, 2)

    def odd(step):
        return step % 2 if isinstance(step, int) else lax.rem(step, 2)

    def reach(step):
        return LINE - 1 - step + inner * (1 - half_of(step)) * (2 * odd(step) - 1)

    def peer(offset):
        return (flipped(offset), core)

    def along(offset):
        return peer(offset * plane)

    def sibling(step):
        return lax.rem(core + step, heads)

    def before(step):
        return lax.rem(core + heads - step, heads)

    def remote(source, target, send, recv, device):
        return pltpu.make_async_remote_copy(
            src_ref=source,
            dst_ref=target,
            send_sem=send,
            recv_sem=recv,
            device_id=device,
            device_id_type=MESH,
        )

    lists = [
        pltpu.make_async_copy(source, target, list_sem.at[position])
        for position, (source, target) in enumerate(
            [(list_hbm, list_ref), (count_hbm, count_ref)]
        )
    ]
    for copy in lists:
        copy.start()
    barrier = pltpu.get_barrier_semaphore()
    for slot in range(1, n):
        pl.semaphore_signal(barrier, inc=1, device_id=peer(slot), device_id_type=MESH)
    for step in range(1, heads):
        pl.semaphore_signal(
            barrier, inc=1, device_id=(me, sibling(step)), device_id_type=MESH
        )

    loads = [
        pltpu.make_async_copy(source, target, load_sem.at[position])
        for position, (source, target) in enumerate(
            [
                (x_hbm, x_vm),
                (qt_hbm, qt_vm),
                (wq_hbm, wq_vm),
                (wk_hbm, wk_vm),
                (wv_hbm, wv_vm),
                (
                    wo_hbm.at[:, pl.ds(pl.multiple_of(core * width, 128), width)],
                    wo_all.at[core],
                ),
            ]
        )
    ]
    for position in (1, 2, 0, 4, 3, 5):
        loads[position].start()

    for copy in lists:
        copy.wait()

    line_shape = (1, ask_vm.shape[1])
    first = lax.broadcasted_iota(jnp.int32, line_shape, 1) * block_count
    number = jnp.zeros(line_shape, jnp.int32)
    flags = [jnp.ones(line_shape, jnp.int32) for _ in range(query_blocks)]
    for block in range(query_blocks):
        count = count_ref[block]
        for entry in range(list_ref.shape[1]):
            distance = list_ref[block, entry] - first
            hit = jnp.logical_and(distance >= 0, distance < block_count)
            unseen = jnp.where(entry < count, 0, 1)
            number = jnp.where(hit, distance, number)
            flags[block] = jnp.minimum(flags[block], jnp.where(hit, unseen, 1))
    ask_vm[0:1] = number
    for block in range(query_blocks):
        ask_vm[block + 1 : block + 2] = flags[block]

    def ask(slot):
        return remote(
            ask_vm, asked_vm.at[slot], ask_send.at[slot], ask_recv.at[slot], peer(slot)
        )

    pl.semaphore_wait(barrier, n - 1 + heads - 1)
    for slot in range(1, n):
        ask(slot).start()

    def token(step, place):
        return remote(
            picked.at[step, place],
            arrived.at[step, place, core],
            tok_send.at[step, place],
            tok_recv.at[step, place],
            peer(place),
        )

    def forward(step, place, hop, part):
        return remote(
            arrived.at[step, place, part],
            arrived.at[step, place, part],
            fwd_send.at[step, place, hop],
            fwd_recv.at[step, place, hop],
            (me, sibling(hop)),
        )

    def weight(hop, part, columns):
        return remote(
            wo_hbm.at[:, pl.ds(pl.multiple_of(columns * width, 128), width)],
            wo_all.at[part],
            wo_send.at[hop],
            wo_recv.at[hop],
            (me, sibling(hop)),
        )

    def context(hop, head, part):
        lanes = pl.ds(head * HEAD_DIM, HEAD_DIM)
        return remote(
            ctx_all.at[part, :, lanes],
            ctx_all.at[part, :, lanes],
            ctx_send.at[hop, head],
            ctx_recv.at[hop, head],
            (me, sibling(hop)),
        )

    routes = [(0, 1, 1), (0, 3, 3), (1, 3, 2), (2, 1, 3), (3, 1, 2)]

    def query(route, head):
        here, to, there = routes[route]
        return remote(
            q_vm.at[here, head],
            q_vm.at[there, head],
            q_send.at[route, head],
            q_recv.at[there, head],
            along(to),
        )

    def query_arrived(slot, head):
        return remote(
            q_vm.at[0, head],
            q_vm.at[slot, head],
            q_send.at[0, head],
            q_recv.at[slot, head],
            along(1),
        )

    def partial(step, slot, to):
        return [
            remote(
                part_out.at[step],
                part_in.at[slot],
                part_send.at[step],
                part_recv.at[slot],
                along(to),
            ),
            remote(
                stat_vm.at[step],
                stat_in.at[slot],
                stat_send.at[step],
                stat_recv.at[slot],
                along(to),
            ),
        ]

    def send(step, slot, to):
        part_out[step] = acc_vm[step].astype(part_out.dtype)
        for copy in partial(step, slot, to):
            copy.start()

    def merge(step, slot):
        for copy in partial(0, slot, 1):
            copy.wait_recv()
        for head in range(head_count):
            lanes = pl.ds(head * HEAD_DIM, HEAD_DIM)
            peak = stat_vm[step, pl.ds(head, 1)]
            other = stat_in[slot, pl.ds(head, 1)]
            top = jnp.maximum(peak, other)
            mine = jnp.exp2(peak - top)
            theirs = jnp.exp2(other - top)
            total = pl.ds(head_count + head, 1)
            stat_vm[step, pl.ds(head, 1)] = top
            stat_vm[step, total] = (
                stat_vm[step, total] * mine + stat_in[slot, total] * theirs
            )
            acc_vm[step, lanes] = acc_vm[step, lanes] * mine + (
                part_in[slot, lanes].astype(jnp.float32) * theirs
            )

    loads[1].wait()
    loads[2].wait()
    for head in range(head_count):
        lanes = pl.ds(head * HEAD_DIM, HEAD_DIM)
        q_vm[0, head] = jnp.dot(
            qt_vm[...], wq_vm[:, lanes], preferred_element_type=jnp.float32
        ).astype(q_vm.dtype)

    for head in range(head_count):
        query(0, head).start()

    @pl.when(inner == 1)
    def _():
        query(1, 0).start()

    loads[0].wait()
    for slot in range(1, n):
        ask(slot).wait_recv()
    asked_vm[0] = ask_vm[...]
    fetch = pltpu.make_async_copy(asked_vm, asked_sm, own_sem.at[0])
    fetch.start()
    fetch.wait()

    def asked(step, place, row, source):
        return asked_sm[reach(step) * plane + place, row, source]

    for step in range(LINE):
        for place in range(1, plane):
            picked[step, place] = x_vm[asked(step, place, 0, me), core]
            token(step, place).start()
    for hop in range(1, heads):
        weight(hop, core, sibling(hop)).start()
    for step in range(LINE):
        arrived[step, 0] = x_vm[asked(step, 0, 0, me)]
    loads[4].wait()
    wvt_vm[...] = wv_vm[...].T
    loads[3].wait()

    @pl.when(inner == 1)
    def _():
        def pass_back(head):
            query_arrived(2, head).wait_recv()
            query(3, head).start()

        for head in range(head_count):
            query_arrived(1, head).wait_recv()
            query(2, head).start()
            if head:
                pass_back(head - 1)
        for head in range(1, head_count):
            query(1, head).start()
        pass_back(head_count - 1)

    half = plane // 2

    def take_in(step, places):
        for place in places:
            if place:
                token(step, place).wait_recv()
                for hop in range(1, heads):
                    forward(step, place, hop, core).start()
        for place in places:
            if place:
                for hop in range(1, heads):
                    forward(step, place, hop, before(hop)).wait_recv()

    def project(step, start):
        tokens = arrived[step, pl.ds(start, half)].reshape(half * BLOCK, depth)
        span = pl.ds(start * BLOCK, half * BLOCK)
        k_vm[span] = jnp.dot(
            tokens, wk_vm[...], preferred_element_type=jnp.float32
        ).astype(k_vm.dtype)
        vt_vm[:, span] = lax.dot_general(
            wvt_vm[...], tokens, NT, preferred_element_type=jnp.float32
        ).astype(vt_vm.dtype)

    def attend(step):
        lane_block = lax.broadcasted_iota(jnp.int32, (1, rows), 1) // BLOCK
        masks = []
        for place in range(plane):
            unseen = jnp.zeros((1, rows), jnp.int32)
            for block in range(query_blocks):
                flag = asked(step, 0, block + 1, flipped(place))
                unseen = jnp.where(lane_block == block, flag, unseen)
            masks.append(unseen.astype(jnp.float32) * HIDDEN)
        for head in range(head_count):
            lanes = pl.ds(head * HEAD_DIM, HEAD_DIM)
            scores = lax.dot_general(
                k_vm[:, lanes],
                q_vm[reach(step), head],
                NT,
                preferred_element_type=jnp.float32,
            )
            scores = [
                scores[place * BLOCK : (place + 1) * BLOCK] + masks[place]
                for place in range(plane)
            ]
            peak = functools.reduce(jnp.maximum, scores)
            peak = jnp.max(peak, axis=0, keepdims=True) * factor
            raised = [jnp.exp2(part * factor - peak) for part in scores]
            total = functools.reduce(jnp.add, raised)
            stat_vm[step, pl.ds(head, 1)] = peak
            stat_vm[step, pl.ds(head_count + head, 1)] = jnp.sum(
                total, axis=0, keepdims=True
            )
            probs = jnp.concatenate([part.astype(vt_vm.dtype) for part in raised], axis=0)
            acc_vm[step, lanes] = jnp.dot(
                vt_vm[lanes], probs, preferred_element_type=jnp.float32
            )

    def one_step(step, carry):
        take_in(step, range(half))
        project(step, 0)
        take_in(step, range(half, plane))
        project(step, half)

        @pl.when(jnp.logical_and(inner == 1, step == 0))
        def _():
            for head in range(head_count):
                query_arrived(3, head).wait_recv()
                query(4, head).start()

        @pl.when(jnp.logical_and(inner == 0, step < LINE - 1))
        def _():
            for head in range(head_count):
                query_arrived(LINE - 1 - step, head).wait_recv()

        attend(step)

        @pl.when(jnp.logical_and(inner == 0, step < LINE - 1))
        def _():
            send(step, step, 1)

        for done in range(1, LINE - 1):

            @pl.when(jnp.logical_and(inner == 1, step == done))
            def _():
                if done == LINE - 2:
                    send(done, 2, 1)
                merge(done - 1, done - 1)
                send(done - 1, 3, done + 1)

        return carry

    lax.fori_loop(0, LINE, one_step, 0)
    last = LINE - 1

    merge(last, 3)
    merge(last, 2)
    for head in range(head_count):
        lanes = pl.ds(head * HEAD_DIM, HEAD_DIM)
        merged = acc_vm[last, lanes] / stat_vm[last, pl.ds(head_count + head, 1)]
        ctx_all[core, :, lanes] = merged.T.astype(ctx_all.dtype)
        for hop in range(1, heads):
            context(hop, head, core).start()
    loads[5].wait()
    result = jnp.dot(ctx_all[core], wo_all[core], preferred_element_type=jnp.float32)
    for hop in range(1, heads):
        part = before(hop)
        weight(hop, part, core).wait_recv()
        for head in range(head_count):
            context(hop, head, part).wait_recv()
        result = result + jnp.dot(
            ctx_all[part], wo_all[part], preferred_element_type=jnp.float32
        )
    out_ref[...] = result.astype(out_ref.dtype)

    for slot in range(1, n):
        ask(slot).wait_send()
    for step in range(LINE):
        for place in range(1, plane):
            token(step, place).wait_send()
            for hop in range(1, heads):
                forward(step, place, hop, core).wait_send()
    for head in range(head_count):
        query(0, head).wait_send()

    @pl.when(inner == 1)
    def _():
        for route in range(1, len(routes)):
            for head in range(head_count):
                query(route, head).wait_send()

    for step in range(LINE - 1):
        for copy in partial(step, 0, 1):
            copy.wait_send()
    for hop in range(1, heads):
        weight(hop, core, sibling(hop)).wait_send()
        for head in range(head_count):
            context(hop, head, core).wait_send()


def per_device(query_tokens, image_tokens, w_query, w_key, w_value, w_out, vis_list, vis_count):
    n = lax.axis_size("view")
    heads = lax.axis_size("head")
    rows, depth = query_tokens.shape
    panel = w_query.shape[1]
    head_count = panel // HEAD_DIM
    width = w_out.shape[1] // heads
    block_count = image_tokens.shape[0] // BLOCK
    part_rows = BLOCK // heads
    query_blocks = vis_list.shape[0]
    plane = n // LINE
    lanes = -(-n // 128) * 128

    anywhere = pl.BlockSpec(memory_space=pltpu.HBM)
    vmem = pl.BlockSpec(memory_space=pltpu.VMEM)
    dtype = image_tokens.dtype
    dma = pltpu.SemaphoreType.DMA
    return pl.pallas_call(
        functools.partial(kernel, n, heads),
        out_shape=jax.ShapeDtypeStruct((rows, width), dtype),
        in_specs=[anywhere] * 8,
        out_specs=vmem,
        scratch_shapes=[
            pltpu.SMEM(vis_list.shape, jnp.int32),
            pltpu.SMEM(vis_count.shape, jnp.int32),
            pltpu.VMEM((block_count, heads, part_rows, depth), dtype),
            pltpu.VMEM((rows, depth), dtype),
            pltpu.VMEM((depth, panel), dtype),
            pltpu.VMEM((depth, panel), dtype),
            pltpu.VMEM((depth, panel), dtype),
            pltpu.VMEM((panel, depth), dtype),
            pltpu.VMEM((heads, panel, width), dtype),
            pltpu.VMEM((1 + query_blocks, lanes), jnp.int32),
            pltpu.VMEM((n, 1 + query_blocks, lanes), jnp.int32),
            pltpu.SMEM((n, 1 + query_blocks, lanes), jnp.int32),
            pltpu.VMEM((LINE, plane, part_rows, depth), dtype),
            pltpu.VMEM((LINE, plane, heads, part_rows, depth), dtype),
            pltpu.VMEM((LINE, head_count, rows, HEAD_DIM), dtype),
            pltpu.VMEM((plane * BLOCK, panel), dtype),
            pltpu.VMEM((panel, plane * BLOCK), dtype),
            pltpu.VMEM((LINE, panel, rows), jnp.float32),
            pltpu.VMEM((LINE, 2 * head_count, rows), jnp.float32),
            pltpu.VMEM((LINE - 1, panel, rows), dtype),
            pltpu.VMEM((LINE, panel, rows), dtype),
            pltpu.VMEM((LINE, 2 * head_count, rows), jnp.float32),
            pltpu.VMEM((heads, rows, panel), dtype),
            dma((2,)),
            dma((6,)),
            dma((n,)),
            dma((n,)),
            dma((1,)),
            dma((LINE, plane)),
            dma((LINE, plane)),
            dma((LINE, plane, heads)),
            dma((LINE, plane, heads)),
            dma((heads,)),
            dma((heads,)),
            dma((5, head_count)),
            dma((LINE, head_count)),
            dma((LINE - 1,)),
            dma((LINE,)),
            dma((LINE - 1,)),
            dma((LINE,)),
            dma((heads, head_count)),
            dma((heads, head_count)),
        ],
        compiler_params=pltpu.CompilerParams(
            collective_id=0, has_side_effects=True, vmem_limit_bytes=int(53.6 * 2**20)
        ),
    )(
        vis_list,
        vis_count,
        image_tokens.reshape(block_count, heads, part_rows, depth),
        query_tokens,
        w_query,
        w_key,
        w_value,
        w_out,
    )


def solution(mesh):
    return jax.shard_map(
        per_device,
        mesh=mesh,
        in_specs=(
            P("view", None),
            P("view", None),
            P(None, "head"),
            P(None, "head"),
            P(None, "head"),
            P("head", None),
            P("view", None),
            P("view"),
        ),
        out_specs=P("view", "head"),
        check_vma=False,
    )
```

```python
import functools
import math

import jax
import jax.numpy as jnp
from jax import lax
from jax.experimental import pallas as pl
from jax.experimental.pallas import tpu as pltpu
from jax.sharding import PartitionSpec as P

HEAD_DIM = 128
BLOCK = 128
LINE = 4
MESH = pl.DeviceIdType.MESH
HIDDEN = -1e30
NT = (((1,), (1,)), ((), ()))


def flipper(index, count):
    changes, bit = [], 1
    while bit < count:
        changes.append((bit, bit - 2 * bit * lax.rem(lax.div(index, bit), 2)))
        bit *= 2

    def flipped(offset):
        result = index
        for bit, change in changes:
            if offset // bit % 2:
                result = result + change
        return result

    return flipped


def kernel(
    n,
    heads,
    list_hbm,
    count_hbm,
    x_hbm,
    qt_hbm,
    wq_hbm,
    wk_hbm,
    wv_hbm,
    wo_hbm,
    out_ref,
    list_ref,
    count_ref,
    x_vm,
    qt_vm,
    wq_vm,
    wk_vm,
    wv_vm,
    wvt_vm,
    wo_all,
    ask_vm,
    asked_vm,
    asked_sm,
    picked,
    arrived,
    q_vm,
    k_vm,
    vt_vm,
    acc_vm,
    stat_vm,
    part_out,
    part_in,
    stat_in,
    ctx_all,
    list_sem,
    load_sem,
    ask_send,
    ask_recv,
    own_sem,
    tok_send,
    tok_recv,
    fwd_send,
    fwd_recv,
    wo_send,
    wo_recv,
    q_send,
    q_recv,
    part_send,
    part_recv,
    stat_send,
    stat_recv,
    ctx_send,
    ctx_recv,
):
    me = lax.axis_index("view")
    core = lax.axis_index("head")
    rows, width = out_ref.shape
    panel = wq_vm.shape[1]
    head_count = panel // HEAD_DIM
    depth = x_vm.shape[-1]
    block_count = x_vm.shape[0]
    plane = n // LINE
    query_blocks = rows // BLOCK
    factor = math.log2(math.e) / math.sqrt(HEAD_DIM)

    level = lax.div(me, plane)
    inner = lax.rem(level + lax.div(level, 2), 2)
    flipped = flipper(me, n)

    def half_of(step):
        return step // 2 if isinstance(step, int) else lax.div(step, 2)

    def odd(step):
        return step % 2 if isinstance(step, int) else lax.rem(step, 2)

    def reach(step):
        return LINE - 1 - step + inner * (1 - half_of(step)) * (2 * odd(step) - 1)

    def peer(offset):
        return (flipped(offset), core)

    def along(offset):
        return peer(offset * plane)

    def sibling(step):
        return lax.rem(core + step, heads)

    def before(step):
        return lax.rem(core + heads - step, heads)

    def remote(source, target, send, recv, device):
        return pltpu.make_async_remote_copy(
            src_ref=source,
            dst_ref=target,
            send_sem=send,
            recv_sem=recv,
            device_id=device,
            device_id_type=MESH,
        )

    lists = [
        pltpu.make_async_copy(source, target, list_sem.at[position])
        for position, (source, target) in enumerate(
            [(list_hbm, list_ref), (count_hbm, count_ref)]
        )
    ]
    for copy in lists:
        copy.start()
    barrier = pltpu.get_barrier_semaphore()
    for slot in range(n - 1, 0, -1):
        pl.semaphore_signal(barrier, inc=1, device_id=peer(slot), device_id_type=MESH)
    for step in range(1, heads):
        pl.semaphore_signal(
            barrier, inc=1, device_id=(me, sibling(step)), device_id_type=MESH
        )

    loads = [
        pltpu.make_async_copy(source, target, load_sem.at[position])
        for position, (source, target) in enumerate(
            [
                (x_hbm, x_vm),
                (qt_hbm, qt_vm),
                (wq_hbm, wq_vm),
                (wk_hbm, wk_vm),
                (wv_hbm, wv_vm),
                (
                    wo_hbm.at[:, pl.ds(pl.multiple_of(core * width, 128), width)],
                    wo_all.at[core],
                ),
            ]
        )
    ]
    for position in (1, 2, 0, 4, 3, 5):
        loads[position].start()

    for copy in lists:
        copy.wait()

    line_shape = (1, ask_vm.shape[1])
    first = lax.broadcasted_iota(jnp.int32, line_shape, 1) * block_count
    number = jnp.zeros(line_shape, jnp.int32)
    flags = [jnp.ones(line_shape, jnp.int32) for _ in range(query_blocks)]
    for block in range(query_blocks):
        count = count_ref[block]
        for entry in range(list_ref.shape[1]):
            distance = list_ref[block, entry] - first
            hit = jnp.logical_and(distance >= 0, distance < block_count)
            unseen = jnp.where(entry < count, 0, 1)
            number = jnp.where(hit, distance, number)
            flags[block] = jnp.minimum(flags[block], jnp.where(hit, unseen, 1))
    ask_vm[0:1] = number
    for block in range(query_blocks):
        ask_vm[block + 1 : block + 2] = flags[block]

    def ask(slot):
        return remote(
            ask_vm, asked_vm.at[slot], ask_send.at[slot], ask_recv.at[slot], peer(slot)
        )

    pl.semaphore_wait(barrier, n - 1 + heads - 1)
    for slot in range(n - 1, 0, -1):
        ask(slot).start()

    def token(step, place):
        return remote(
            picked.at[step, place],
            arrived.at[step, place, core],
            tok_send.at[step, place],
            tok_recv.at[step, place],
            peer(place),
        )

    def forward(step, place, hop, part):
        return remote(
            arrived.at[step, place, part],
            arrived.at[step, place, part],
            fwd_send.at[step, place, hop],
            fwd_recv.at[step, place, hop],
            (me, sibling(hop)),
        )

    def weight(hop, part, columns):
        return remote(
            wo_hbm.at[:, pl.ds(pl.multiple_of(columns * width, 128), width)],
            wo_all.at[part],
            wo_send.at[hop],
            wo_recv.at[hop],
            (me, sibling(hop)),
        )

    def context(hop, head, part):
        lanes = pl.ds(head * HEAD_DIM, HEAD_DIM)
        return remote(
            ctx_all.at[part, :, lanes],
            ctx_all.at[part, :, lanes],
            ctx_send.at[hop, head],
            ctx_recv.at[hop, head],
            (me, sibling(hop)),
        )

    routes = [(0, 1, 1), (0, 3, 3), (1, 3, 2), (2, 1, 3), (3, 1, 2)]

    def query(route, head):
        here, to, there = routes[route]
        return remote(
            q_vm.at[here, head],
            q_vm.at[there, head],
            q_send.at[route, head],
            q_recv.at[there, head],
            along(to),
        )

    def query_arrived(slot, head):
        return remote(
            q_vm.at[0, head],
            q_vm.at[slot, head],
            q_send.at[0, head],
            q_recv.at[slot, head],
            along(1),
        )

    def partial(step, slot, to, head):
        lanes = pl.ds(head * HEAD_DIM, HEAD_DIM)
        return remote(
            part_out.at[step, lanes],
            part_in.at[slot, lanes],
            part_send.at[step, head],
            part_recv.at[slot, head],
            along(to),
        )

    def stats(step, slot, to, head):
        return remote(
            stat_vm.at[step, head],
            stat_in.at[slot, head],
            stat_send.at[step, head],
            stat_recv.at[slot, head],
            along(to),
        )

    def merge(step, slot, head, to=None, there=None):
        lanes = pl.ds(head * HEAD_DIM, HEAD_DIM)
        stats(0, slot, 1, head).wait_recv()
        partial(0, slot, 1, head).wait_recv()
        peak, other = stat_vm[step, head, 0:1], stat_in[slot, head, 0:1]
        top = jnp.maximum(peak, other)
        mine = jnp.exp2(peak - top)
        theirs = jnp.exp2(other - top)
        stat_vm[step, head, 0:1] = top
        stat_vm[step, head, 1:2] = (
            stat_vm[step, head, 1:2] * mine + stat_in[slot, head, 1:2] * theirs
        )
        both = acc_vm[step, lanes] * mine + (
            part_in[slot, lanes].astype(jnp.float32) * theirs
        )
        if to is None:
            acc_vm[step, lanes] = both
        else:
            part_out[step, lanes] = both.astype(part_out.dtype)
            stats(step, there, to, head).start()
            partial(step, there, to, head).start()

    loads[1].wait()
    loads[2].wait()
    for head in range(head_count):
        lanes = pl.ds(head * HEAD_DIM, HEAD_DIM)
        q_vm[0, head] = jnp.dot(
            qt_vm[...], wq_vm[:, lanes], preferred_element_type=jnp.float32
        ).astype(q_vm.dtype)

    for head in range(head_count):
        query(0, head).start()

    early = head_count - head_count // 2

    @pl.when(inner == 1)
    def _():
        for head in range(early):
            query(1, head).start()

    loads[0].wait()
    for slot in range(1, n):
        ask(slot).wait_recv()
    asked_vm[0] = ask_vm[...]
    fetch = pltpu.make_async_copy(asked_vm, asked_sm, own_sem.at[0])
    fetch.start()

    def asked(step, place, row, source):
        return asked_sm[reach(step) * plane + place, row, source]

    lane = lax.broadcasted_iota(jnp.int32, (1, ask_vm.shape[1]), 1)

    def wanted(step, place):
        row = asked_vm[reach(step) * plane + place, 0:1]
        return jnp.max(jnp.where(lane == me, row, 0))

    blocks = [[wanted(step, place) for place in range(plane)] for step in range(LINE)]
    for step in range(LINE):
        for place in range(1, plane):
            picked[step, place] = x_vm[blocks[step][place], core]
            token(step, place).start()
    @pl.when(inner == 1)
    def _():
        for head in range(head_count):
            query_arrived(1, head).wait_recv()
            query(2, head).start()
        for head in range(early, head_count):
            query(1, head).start()

    for hop in range(1, heads):
        weight(hop, core, sibling(hop)).start()
    for step in range(LINE):
        arrived[step, 0] = x_vm[blocks[step][0]]
    fetch.wait()
    loads[4].wait()
    wvt_vm[...] = wv_vm[...].T
    loads[3].wait()

    @pl.when(inner == 1)
    def _():
        for head in range(head_count):
            query_arrived(2, head).wait_recv()
            query(3, head).start()
        for head in range(early):
            query_arrived(3, head).wait_recv()
            query(4, head).start()

    late = plane - plane // 4 if plane >= 4 else plane - 1
    sooner, later = range(late), range(late, plane)

    def hand_over(step, places):
        for place in places:
            if place:
                token(step, place).wait_recv()
                for hop in range(1, heads):
                    forward(step, place, hop, core).start()

    def settle(step, places):
        for place in places:
            if place:
                for hop in range(1, heads):
                    forward(step, place, hop, before(hop)).wait_recv()

    def project(step, places):
        start, size = places[0], len(places)
        tokens = arrived[step, pl.ds(start, size)].reshape(size * BLOCK, depth)
        span = pl.ds(start * BLOCK, size * BLOCK)
        k_vm[span] = jnp.dot(
            tokens, wk_vm[...], preferred_element_type=jnp.float32
        ).astype(k_vm.dtype)
        vt_vm[:, span] = lax.dot_general(
            wvt_vm[...], tokens, NT, preferred_element_type=jnp.float32
        ).astype(vt_vm.dtype)

    def give(step, head):
        lanes = pl.ds(head * HEAD_DIM, HEAD_DIM)
        part_out[step, lanes] = acc_vm[step, lanes].astype(part_out.dtype)
        stats(step, step, 1, head).start()
        partial(step, step, 1, head).start()

    def attend(step, following=None):
        lane_block = lax.broadcasted_iota(jnp.int32, (1, rows), 1) // BLOCK
        masks = []
        for place in range(plane):
            unseen = jnp.zeros((1, rows), jnp.int32)
            for block in range(query_blocks):
                flag = asked(step, 0, block + 1, flipped(place))
                unseen = jnp.where(lane_block == block, flag, unseen)
            masks.append(unseen.astype(jnp.float32) * HIDDEN)
        for head in range(head_count):
            if following is not None and head == head_count // 2:
                hand_over(following, sooner)
            lanes = pl.ds(head * HEAD_DIM, HEAD_DIM)
            scores = lax.dot_general(
                k_vm[:, lanes],
                q_vm[reach(step), head],
                NT,
                preferred_element_type=jnp.float32,
            )
            scores = [
                scores[place * BLOCK : (place + 1) * BLOCK] + masks[place]
                for place in range(plane)
            ]
            peak = functools.reduce(jnp.maximum, scores)
            peak = jnp.max(peak, axis=0, keepdims=True) * factor
            raised = [jnp.exp2(part * factor - peak) for part in scores]
            total = functools.reduce(jnp.add, raised)
            stat_vm[step, head, 0:1] = peak
            stat_vm[step, head, 1:2] = jnp.sum(total, axis=0, keepdims=True)
            probs = jnp.concatenate([part.astype(vt_vm.dtype) for part in raised], axis=0)
            acc_vm[step, lanes] = jnp.dot(
                vt_vm[lanes], probs, preferred_element_type=jnp.float32
            )

    def collect(step):
        settle(step, sooner)
        project(step, sooner)
        hand_over(step, later)
        settle(step, later)
        project(step, later)

    def tokens_sent(step):
        for place in range(1, plane):
            token(step, place).wait_send()
            for hop in range(1, heads):
                forward(step, place, hop, core).wait_send()

    def far_step(step, carry):
        collect(step)

        @pl.when(jnp.logical_and(inner == 1, step == 0))
        def _():
            for head in range(early, head_count):
                query_arrived(3, head).wait_recv()
                query(4, head).start()

        @pl.when(inner == 0)
        def _():
            for head in range(head_count):
                query_arrived(LINE - 1 - step, head).wait_recv()

        attend(step, step + 1)

        @pl.when(inner == 0)
        def _():
            for head in range(head_count):
                give(step, head)

        return carry

    hand_over(0, sooner)
    lax.fori_loop(0, LINE - 2, far_step, 0)
    near, last = LINE - 2, LINE - 1

    @pl.when(inner == 1)
    def _():
        for head in range(head_count):
            merge(0, 0, head, 3, 3)

    for slot in range(1, n):
        ask(slot).wait_send()
    for step in range(near):
        tokens_sent(step)
    for head in range(head_count):
        query(0, head).wait_send()
    collect(near)

    @pl.when(inner == 0)
    def _():
        for head in range(head_count):
            query_arrived(1, head).wait_recv()

    attend(near, last)

    @pl.when(inner == 0)
    def _():
        for head in range(head_count):
            give(near, head)

    @pl.when(inner == 1)
    def _():
        for head in range(head_count):
            merge(near, 3, head, 1, 2)
            merge(1, 1, head, 3, 4)
        for route in range(1, len(routes)):
            for head in range(head_count):
                query(route, head).wait_send()

    tokens_sent(near)
    for hop in range(1, heads):
        weight(hop, core, sibling(hop)).wait_send()
        weight(hop, before(hop), core).wait_recv()
    loads[5].wait()
    collect(last)
    attend(last)

    @pl.when(inner == 1)
    def _():
        for head in range(head_count):
            merge(last, 4, head)

    for head in range(head_count):
        lanes = pl.ds(head * HEAD_DIM, HEAD_DIM)
        merge(last, 2, head)
        merged = acc_vm[last, lanes] / stat_vm[last, head, 1:2]
        ctx_all[core, :, lanes] = merged.T.astype(ctx_all.dtype)
        for hop in range(1, heads):
            context(hop, head, core).start()
    result = jnp.dot(ctx_all[core], wo_all[core], preferred_element_type=jnp.float32)
    for hop in range(1, heads):
        part = before(hop)
        for head in range(head_count):
            context(hop, head, part).wait_recv()
        result = result + jnp.dot(
            ctx_all[part], wo_all[part], preferred_element_type=jnp.float32
        )
    out_ref[...] = result.astype(out_ref.dtype)

    tokens_sent(last)
    for step in range(LINE - 1):
        for head in range(head_count):
            stats(step, 0, 1, head).wait_send()
            partial(step, 0, 1, head).wait_send()
    for hop in range(1, heads):
        for head in range(head_count):
            context(hop, head, core).wait_send()


def per_device(query_tokens, image_tokens, w_query, w_key, w_value, w_out, vis_list, vis_count):
    n = lax.axis_size("view")
    heads = lax.axis_size("head")
    rows, depth = query_tokens.shape
    panel = w_query.shape[1]
    head_count = panel // HEAD_DIM
    width = w_out.shape[1] // heads
    block_count = image_tokens.shape[0] // BLOCK
    part_rows = BLOCK // heads
    query_blocks = vis_list.shape[0]
    plane = n // LINE
    lanes = -(-n // 128) * 128

    anywhere = pl.BlockSpec(memory_space=pltpu.HBM)
    vmem = pl.BlockSpec(memory_space=pltpu.VMEM)
    dtype = image_tokens.dtype
    dma = pltpu.SemaphoreType.DMA
    return pl.pallas_call(
        functools.partial(kernel, n, heads),
        out_shape=jax.ShapeDtypeStruct((rows, width), dtype),
        in_specs=[anywhere] * 8,
        out_specs=vmem,
        scratch_shapes=[
            pltpu.SMEM(vis_list.shape, jnp.int32),
            pltpu.SMEM(vis_count.shape, jnp.int32),
            pltpu.VMEM((block_count, heads, part_rows, depth), dtype),
            pltpu.VMEM((rows, depth), dtype),
            pltpu.VMEM((depth, panel), dtype),
            pltpu.VMEM((depth, panel), dtype),
            pltpu.VMEM((depth, panel), dtype),
            pltpu.VMEM((panel, depth), dtype),
            pltpu.VMEM((heads, panel, width), dtype),
            pltpu.VMEM((1 + query_blocks, lanes), jnp.int32),
            pltpu.VMEM((n, 1 + query_blocks, lanes), jnp.int32),
            pltpu.SMEM((n, 1 + query_blocks, lanes), jnp.int32),
            pltpu.VMEM((LINE, plane, part_rows, depth), dtype),
            pltpu.VMEM((LINE, plane, heads, part_rows, depth), dtype),
            pltpu.VMEM((LINE, head_count, rows, HEAD_DIM), dtype),
            pltpu.VMEM((plane * BLOCK, panel), dtype),
            pltpu.VMEM((panel, plane * BLOCK), dtype),
            pltpu.VMEM((LINE, panel, rows), jnp.float32),
            pltpu.VMEM((LINE, head_count, 2, rows), jnp.float32),
            pltpu.VMEM((LINE - 1, panel, rows), dtype),
            pltpu.VMEM((5, panel, rows), dtype),
            pltpu.VMEM((5, head_count, 2, rows), jnp.float32),
            pltpu.VMEM((heads, rows, panel), dtype),
            dma((2,)),
            dma((6,)),
            dma((n,)),
            dma((n,)),
            dma((1,)),
            dma((LINE, plane)),
            dma((LINE, plane)),
            dma((LINE, plane, heads)),
            dma((LINE, plane, heads)),
            dma((heads,)),
            dma((heads,)),
            dma((5, head_count)),
            dma((LINE, head_count)),
            dma((LINE - 1, head_count)),
            dma((5, head_count)),
            dma((LINE - 1, head_count)),
            dma((5, head_count)),
            dma((heads, head_count)),
            dma((heads, head_count)),
        ],
        compiler_params=pltpu.CompilerParams(
            collective_id=0, has_side_effects=True, vmem_limit_bytes=int(53.6 * 2**20)
        ),
    )(
        vis_list,
        vis_count,
        image_tokens.reshape(block_count, heads, part_rows, depth),
        query_tokens,
        w_query,
        w_key,
        w_value,
        w_out,
    )


def solution(mesh):
    return jax.shard_map(
        per_device,
        mesh=mesh,
        in_specs=(
            P("view", None),
            P("view", None),
            P(None, "head"),
            P(None, "head"),
            P(None, "head"),
            P("head", None),
            P("view", None),
            P("view"),
        ),
        out_specs=P("view", "head"),
        check_vma=False,
    )
```

```python
import functools
import math

import jax
import jax.numpy as jnp
from jax import lax
from jax.experimental import pallas as pl
from jax.experimental.pallas import tpu as pltpu
from jax.sharding import PartitionSpec as P

HEAD_DIM = 128
BLOCK = 128
LINE = 4
MESH = pl.DeviceIdType.MESH
HIDDEN = -1e30
NT = (((1,), (1,)), ((), ()))


def flipper(index, count):
    changes, bit = [], 1
    while bit < count:
        changes.append((bit, bit - 2 * bit * lax.rem(lax.div(index, bit), 2)))
        bit *= 2

    def flipped(offset):
        result = index
        for bit, change in changes:
            if offset // bit % 2:
                result = result + change
        return result

    return flipped


def kernel(
    n,
    heads,
    list_hbm,
    count_hbm,
    x_hbm,
    qt_hbm,
    wq_hbm,
    wk_hbm,
    wv_hbm,
    wo_hbm,
    out_ref,
    list_ref,
    count_ref,
    x_vm,
    qt_vm,
    wq_vm,
    wk_vm,
    wv_vm,
    wvt_vm,
    wo_all,
    ask_vm,
    asked_vm,
    asked_sm,
    picked,
    arrived,
    q_vm,
    k_vm,
    vt_vm,
    acc_vm,
    stat_vm,
    part_out,
    part_in,
    stat_in,
    ctx_all,
    list_sem,
    load_sem,
    ask_send,
    ask_recv,
    own_sem,
    tok_send,
    tok_recv,
    fwd_send,
    fwd_recv,
    wo_send,
    wo_recv,
    q_send,
    q_recv,
    part_send,
    part_recv,
    stat_send,
    stat_recv,
    ctx_send,
    ctx_recv,
):
    me = lax.axis_index("view")
    core = lax.axis_index("head")
    rows, width = out_ref.shape
    panel = wq_vm.shape[1]
    head_count = panel // HEAD_DIM
    depth = x_vm.shape[-1]
    block_count = x_vm.shape[0]
    plane = n // LINE
    query_blocks = rows // BLOCK
    factor = math.log2(math.e) / math.sqrt(HEAD_DIM)

    level = lax.div(me, plane)
    inner = lax.rem(level + lax.div(level, 2), 2)
    flipped = flipper(me, n)

    def half_of(step):
        return step // 2 if isinstance(step, int) else lax.div(step, 2)

    def odd(step):
        return step % 2 if isinstance(step, int) else lax.rem(step, 2)

    def reach(step):
        return LINE - 1 - step + inner * (1 - half_of(step)) * (2 * odd(step) - 1)

    def peer(offset):
        return (flipped(offset), core)

    def along(offset):
        return peer(offset * plane)

    def sibling(step):
        return lax.rem(core + step, heads)

    def before(step):
        return lax.rem(core + heads - step, heads)

    def remote(source, target, send, recv, device):
        return pltpu.make_async_remote_copy(
            src_ref=source,
            dst_ref=target,
            send_sem=send,
            recv_sem=recv,
            device_id=device,
            device_id_type=MESH,
        )

    lists = [
        pltpu.make_async_copy(source, target, list_sem.at[position])
        for position, (source, target) in enumerate(
            [(list_hbm, list_ref), (count_hbm, count_ref)]
        )
    ]
    for copy in lists:
        copy.start()
    barrier = pltpu.get_barrier_semaphore()
    for slot in range(n - 1, 0, -1):
        pl.semaphore_signal(barrier, inc=1, device_id=peer(slot), device_id_type=MESH)
    for step in range(1, heads):
        pl.semaphore_signal(
            barrier, inc=1, device_id=(me, sibling(step)), device_id_type=MESH
        )

    loads = [
        pltpu.make_async_copy(source, target, load_sem.at[position])
        for position, (source, target) in enumerate(
            [
                (x_hbm, x_vm),
                (qt_hbm, qt_vm),
                (wq_hbm, wq_vm),
                (wk_hbm, wk_vm),
                (wv_hbm, wv_vm),
                (
                    wo_hbm.at[:, pl.ds(pl.multiple_of(core * width, 128), width)],
                    wo_all.at[core],
                ),
            ]
        )
    ]
    for position in (1, 2, 0, 4, 3, 5):
        loads[position].start()

    for copy in lists:
        copy.wait()

    line_shape = (1, ask_vm.shape[1])
    first = lax.broadcasted_iota(jnp.int32, line_shape, 1) * block_count
    number = jnp.zeros(line_shape, jnp.int32)
    flags = [jnp.ones(line_shape, jnp.int32) for _ in range(query_blocks)]
    for block in range(query_blocks):
        count = count_ref[block]
        for entry in range(list_ref.shape[1]):
            distance = list_ref[block, entry] - first
            hit = jnp.logical_and(distance >= 0, distance < block_count)
            unseen = jnp.where(entry < count, 0, 1)
            number = jnp.where(hit, distance, number)
            flags[block] = jnp.minimum(flags[block], jnp.where(hit, unseen, 1))
    ask_vm[0:1] = number
    for block in range(query_blocks):
        ask_vm[block + 1 : block + 2] = flags[block]

    def ask(slot):
        return remote(
            ask_vm, asked_vm.at[slot], ask_send.at[slot], ask_recv.at[slot], peer(slot)
        )

    pl.semaphore_wait(barrier, n - 1 + heads - 1)
    for slot in range(n - 1, 0, -1):
        ask(slot).start()

    def token(step, place):
        return remote(
            picked.at[step, place],
            arrived.at[step, place, core],
            tok_send.at[step, place],
            tok_recv.at[step, place],
            peer(place),
        )

    def forward(step, place, hop, part):
        return remote(
            arrived.at[step, place, part],
            arrived.at[step, place, part],
            fwd_send.at[step, place, hop],
            fwd_recv.at[step, place, hop],
            (me, sibling(hop)),
        )

    def weight(hop, part, columns):
        return remote(
            wo_hbm.at[:, pl.ds(pl.multiple_of(columns * width, 128), width)],
            wo_all.at[part],
            wo_send.at[hop],
            wo_recv.at[hop],
            (me, sibling(hop)),
        )

    def context(hop, head, part):
        lanes = pl.ds(head * HEAD_DIM, HEAD_DIM)
        return remote(
            ctx_all.at[part, :, lanes],
            ctx_all.at[part, :, lanes],
            ctx_send.at[hop, head],
            ctx_recv.at[hop, head],
            (me, sibling(hop)),
        )

    routes = [(0, 1, 1), (0, 3, 3), (1, 3, 2), (2, 1, 3), (3, 1, 2)]

    def query(route, head):
        here, to, there = routes[route]
        return remote(
            q_vm.at[here, head],
            q_vm.at[there, head],
            q_send.at[route, head],
            q_recv.at[there, head],
            along(to),
        )

    def query_arrived(slot, head):
        return remote(
            q_vm.at[0, head],
            q_vm.at[slot, head],
            q_send.at[0, head],
            q_recv.at[slot, head],
            along(1),
        )

    def partial(step, slot, to, head):
        lanes = pl.ds(head * HEAD_DIM, HEAD_DIM)
        return remote(
            part_out.at[step, lanes],
            part_in.at[slot, lanes],
            part_send.at[step, head],
            part_recv.at[slot, head],
            along(to),
        )

    def stats(step, slot, to, head):
        return remote(
            stat_vm.at[step, head],
            stat_in.at[slot, head],
            stat_send.at[step, head],
            stat_recv.at[slot, head],
            along(to),
        )

    def merge(step, slot, head, to=None, there=None):
        lanes = pl.ds(head * HEAD_DIM, HEAD_DIM)
        stats(0, slot, 1, head).wait_recv()
        partial(0, slot, 1, head).wait_recv()
        peak, other = stat_vm[step, head, 0:1], stat_in[slot, head, 0:1]
        top = jnp.maximum(peak, other)
        mine = jnp.exp2(peak - top)
        theirs = jnp.exp2(other - top)
        stat_vm[step, head, 0:1] = top
        stat_vm[step, head, 1:2] = (
            stat_vm[step, head, 1:2] * mine + stat_in[slot, head, 1:2] * theirs
        )
        both = acc_vm[step, lanes] * mine + (
            part_in[slot, lanes].astype(jnp.float32) * theirs
        )
        if to is None:
            acc_vm[step, lanes] = both
        else:
            part_out[step, lanes] = both.astype(part_out.dtype)
            stats(step, there, to, head).start()
            partial(step, there, to, head).start()

    loads[1].wait()
    loads[2].wait()
    for head in range(head_count):
        lanes = pl.ds(head * HEAD_DIM, HEAD_DIM)
        q_vm[0, head] = jnp.dot(
            qt_vm[...], wq_vm[:, lanes], preferred_element_type=jnp.float32
        ).astype(q_vm.dtype)
        query(0, head).start()

    early = head_count - head_count // 2

    @pl.when(inner == 1)
    def _():
        for head in range(early):
            query(1, head).start()

    loads[0].wait()
    for slot in range(1, n):
        ask(slot).wait_recv()
    asked_vm[0] = ask_vm[...]
    fetch = pltpu.make_async_copy(asked_vm, asked_sm, own_sem.at[0])
    fetch.start()

    def asked(step, place, row, source):
        return asked_sm[reach(step) * plane + place, row, source]

    lane = lax.broadcasted_iota(jnp.int32, (1, ask_vm.shape[1]), 1)

    def wanted(step, place):
        row = asked_vm[reach(step) * plane + place, 0:1]
        return jnp.max(jnp.where(lane == me, row, 0))

    blocks = [[wanted(step, place) for place in range(plane)] for step in range(LINE)]
    for step in range(LINE):
        for place in range(1, plane):
            picked[step, place] = x_vm[blocks[step][place], core]
            token(step, place).start()
    @pl.when(inner == 1)
    def _():
        for head in range(head_count):
            query_arrived(1, head).wait_recv()
            query(2, head).start()
        for head in range(early, head_count):
            query(1, head).start()

    for hop in range(1, heads):
        weight(hop, core, sibling(hop)).start()
    for step in range(LINE):
        arrived[step, 0] = x_vm[blocks[step][0]]
    fetch.wait()
    loads[4].wait()
    wvt_vm[...] = wv_vm[...].T
    loads[3].wait()

    late = plane - plane // 4 if plane >= 4 else plane - 1
    sooner, later = range(late), range(late, plane)

    def hand_over(step, places):
        for place in places:
            if place:
                token(step, place).wait_recv()
                for hop in range(1, heads):
                    forward(step, place, hop, core).start()

    def settle(step, places):
        for place in places:
            if place:
                for hop in range(1, heads):
                    forward(step, place, hop, before(hop)).wait_recv()

    def project(step, places):
        start, size = places[0], len(places)
        tokens = arrived[step, pl.ds(start, size)].reshape(size * BLOCK, depth)
        span = pl.ds(start * BLOCK, size * BLOCK)
        k_vm[span] = jnp.dot(
            tokens, wk_vm[...], preferred_element_type=jnp.float32
        ).astype(k_vm.dtype)
        vt_vm[:, span] = lax.dot_general(
            wvt_vm[...], tokens, NT, preferred_element_type=jnp.float32
        ).astype(vt_vm.dtype)

    def give(step, head):
        lanes = pl.ds(head * HEAD_DIM, HEAD_DIM)
        part_out[step, lanes] = acc_vm[step, lanes].astype(part_out.dtype)
        stats(step, step, 1, head).start()
        partial(step, step, 1, head).start()

    def attend(step, following=None):
        lane_block = lax.broadcasted_iota(jnp.int32, (1, rows), 1) // BLOCK
        masks = []
        for place in range(plane):
            unseen = jnp.zeros((1, rows), jnp.int32)
            for block in range(query_blocks):
                flag = asked(step, 0, block + 1, flipped(place))
                unseen = jnp.where(lane_block == block, flag, unseen)
            masks.append(unseen.astype(jnp.float32) * HIDDEN)
        for head in range(head_count):
            if following is not None and head == head_count // 2:
                hand_over(following, sooner)
            lanes = pl.ds(head * HEAD_DIM, HEAD_DIM)
            scores = lax.dot_general(
                k_vm[:, lanes],
                q_vm[reach(step), head],
                NT,
                preferred_element_type=jnp.float32,
            )
            scores = [
                scores[place * BLOCK : (place + 1) * BLOCK] + masks[place]
                for place in range(plane)
            ]
            peak = functools.reduce(jnp.maximum, scores)
            peak = jnp.max(peak, axis=0, keepdims=True) * factor
            raised = [jnp.exp2(part * factor - peak) for part in scores]
            total = functools.reduce(jnp.add, raised)
            stat_vm[step, head, 0:1] = peak
            stat_vm[step, head, 1:2] = jnp.sum(total, axis=0, keepdims=True)
            probs = jnp.concatenate([part.astype(vt_vm.dtype) for part in raised], axis=0)
            acc_vm[step, lanes] = jnp.dot(
                vt_vm[lanes], probs, preferred_element_type=jnp.float32
            )

    def collect(step):
        settle(step, sooner)
        project(step, sooner)
        hand_over(step, later)
        settle(step, later)
        project(step, later)

    def tokens_sent(step):
        for place in range(1, plane):
            token(step, place).wait_send()
            for hop in range(1, heads):
                forward(step, place, hop, core).wait_send()

    def far_step(step, carry):
        collect(step)

        @pl.when(jnp.logical_and(inner == 1, step == 0))
        def _():
            for head in range(early, head_count):
                query_arrived(3, head).wait_recv()
                query(4, head).start()

        @pl.when(inner == 0)
        def _():
            for head in range(head_count):
                query_arrived(LINE - 1 - step, head).wait_recv()

        attend(step, step + 1)

        @pl.when(inner == 0)
        def _():
            for head in range(head_count):
                give(step, head)

        return carry

    def pass_back(heads_now):
        for head in heads_now:
            query_arrived(2, head).wait_recv()
            query(3, head).start()

    @pl.when(inner == 1)
    def _():
        pass_back(range(early))

    hand_over(0, sooner)

    @pl.when(inner == 1)
    def _():
        pass_back(range(early, head_count))
        for head in range(early):
            query_arrived(3, head).wait_recv()
            query(4, head).start()

    lax.fori_loop(0, LINE - 2, far_step, 0)
    near, last = LINE - 2, LINE - 1

    @pl.when(inner == 1)
    def _():
        for head in range(head_count):
            merge(0, 0, head, 3, 3)

    for slot in range(1, n):
        ask(slot).wait_send()
    for step in range(near):
        tokens_sent(step)
    for head in range(head_count):
        query(0, head).wait_send()
    collect(near)

    @pl.when(inner == 0)
    def _():
        for head in range(head_count):
            query_arrived(1, head).wait_recv()

    attend(near, last)

    @pl.when(inner == 0)
    def _():
        for head in range(head_count):
            give(near, head)

    @pl.when(inner == 1)
    def _():
        for head in range(head_count):
            merge(near, 3, head, 1, 2)
            merge(1, 1, head, 3, 4)
        for route in range(1, len(routes)):
            for head in range(head_count):
                query(route, head).wait_send()

    tokens_sent(near)
    for hop in range(1, heads):
        weight(hop, core, sibling(hop)).wait_send()
        weight(hop, before(hop), core).wait_recv()
    loads[5].wait()
    collect(last)
    attend(last)

    @pl.when(inner == 1)
    def _():
        for head in range(head_count):
            merge(last, 4, head)

    for head in range(head_count):
        lanes = pl.ds(head * HEAD_DIM, HEAD_DIM)
        merge(last, 2, head)
        merged = acc_vm[last, lanes] / stat_vm[last, head, 1:2]
        ctx_all[core, :, lanes] = merged.T.astype(ctx_all.dtype)
        for hop in range(1, heads):
            context(hop, head, core).start()
    result = jnp.dot(ctx_all[core], wo_all[core], preferred_element_type=jnp.float32)
    for hop in range(1, heads):
        part = before(hop)
        for head in range(head_count):
            context(hop, head, part).wait_recv()
        result = result + jnp.dot(
            ctx_all[part], wo_all[part], preferred_element_type=jnp.float32
        )
    out_ref[...] = result.astype(out_ref.dtype)

    tokens_sent(last)
    for step in range(LINE - 1):
        for head in range(head_count):
            stats(step, 0, 1, head).wait_send()
            partial(step, 0, 1, head).wait_send()
    for hop in range(1, heads):
        for head in range(head_count):
            context(hop, head, core).wait_send()


def per_device(query_tokens, image_tokens, w_query, w_key, w_value, w_out, vis_list, vis_count):
    n = lax.axis_size("view")
    heads = lax.axis_size("head")
    rows, depth = query_tokens.shape
    panel = w_query.shape[1]
    head_count = panel // HEAD_DIM
    width = w_out.shape[1] // heads
    block_count = image_tokens.shape[0] // BLOCK
    part_rows = BLOCK // heads
    query_blocks = vis_list.shape[0]
    plane = n // LINE
    lanes = -(-n // 128) * 128

    anywhere = pl.BlockSpec(memory_space=pltpu.HBM)
    vmem = pl.BlockSpec(memory_space=pltpu.VMEM)
    dtype = image_tokens.dtype
    dma = pltpu.SemaphoreType.DMA
    return pl.pallas_call(
        functools.partial(kernel, n, heads),
        out_shape=jax.ShapeDtypeStruct((rows, width), dtype),
        in_specs=[anywhere] * 8,
        out_specs=vmem,
        scratch_shapes=[
            pltpu.SMEM(vis_list.shape, jnp.int32),
            pltpu.SMEM(vis_count.shape, jnp.int32),
            pltpu.VMEM((block_count, heads, part_rows, depth), dtype),
            pltpu.VMEM((rows, depth), dtype),
            pltpu.VMEM((depth, panel), dtype),
            pltpu.VMEM((depth, panel), dtype),
            pltpu.VMEM((depth, panel), dtype),
            pltpu.VMEM((panel, depth), dtype),
            pltpu.VMEM((heads, panel, width), dtype),
            pltpu.VMEM((1 + query_blocks, lanes), jnp.int32),
            pltpu.VMEM((n, 1 + query_blocks, lanes), jnp.int32),
            pltpu.SMEM((n, 1 + query_blocks, lanes), jnp.int32),
            pltpu.VMEM((LINE, plane, part_rows, depth), dtype),
            pltpu.VMEM((LINE, plane, heads, part_rows, depth), dtype),
            pltpu.VMEM((LINE, head_count, rows, HEAD_DIM), dtype),
            pltpu.VMEM((plane * BLOCK, panel), dtype),
            pltpu.VMEM((panel, plane * BLOCK), dtype),
            pltpu.VMEM((LINE, panel, rows), jnp.float32),
            pltpu.VMEM((LINE, head_count, 2, rows), jnp.float32),
            pltpu.VMEM((LINE - 1, panel, rows), dtype),
            pltpu.VMEM((5, panel, rows), dtype),
            pltpu.VMEM((5, head_count, 2, rows), jnp.float32),
            pltpu.VMEM((heads, rows, panel), dtype),
            dma((2,)),
            dma((6,)),
            dma((n,)),
            dma((n,)),
            dma((1,)),
            dma((LINE, plane)),
            dma((LINE, plane)),
            dma((LINE, plane, heads)),
            dma((LINE, plane, heads)),
            dma((heads,)),
            dma((heads,)),
            dma((5, head_count)),
            dma((LINE, head_count)),
            dma((LINE - 1, head_count)),
            dma((5, head_count)),
            dma((LINE - 1, head_count)),
            dma((5, head_count)),
            dma((heads, head_count)),
            dma((heads, head_count)),
        ],
        compiler_params=pltpu.CompilerParams(
            collective_id=0, has_side_effects=True, vmem_limit_bytes=int(53.6 * 2**20)
        ),
    )(
        vis_list,
        vis_count,
        image_tokens.reshape(block_count, heads, part_rows, depth),
        query_tokens,
        w_query,
        w_key,
        w_value,
        w_out,
    )


def solution(mesh):
    return jax.shard_map(
        per_device,
        mesh=mesh,
        in_specs=(
            P("view", None),
            P("view", None),
            P(None, "head"),
            P(None, "head"),
            P(None, "head"),
            P("head", None),
            P("view", None),
            P("view"),
        ),
        out_specs=P("view", "head"),
        check_vma=False,
    )
```

```python
import functools
import math

import jax
import jax.numpy as jnp
from jax import lax
from jax.experimental import pallas as pl
from jax.experimental.pallas import tpu as pltpu
from jax.sharding import PartitionSpec as P

HEAD_DIM = 128
BLOCK = 128
LINE = 4
MESH = pl.DeviceIdType.MESH
HIDDEN = -1e30
NT = (((1,), (1,)), ((), ()))


def flipper(index, count):
    changes, bit = [], 1
    while bit < count:
        changes.append((bit, bit - 2 * bit * lax.rem(lax.div(index, bit), 2)))
        bit *= 2

    def flipped(offset):
        result = index
        for bit, change in changes:
            if offset // bit % 2:
                result = result + change
        return result

    return flipped


def kernel(
    n,
    heads,
    list_hbm,
    count_hbm,
    x_hbm,
    qt_hbm,
    wq_hbm,
    wk_hbm,
    wv_hbm,
    wo_hbm,
    out_ref,
    list_ref,
    count_ref,
    x_vm,
    qt_vm,
    wq_vm,
    wk_vm,
    wv_vm,
    wvt_vm,
    wo_all,
    ask_vm,
    asked_vm,
    asked_sm,
    picked,
    arrived,
    q_vm,
    k_vm,
    vt_vm,
    acc_vm,
    stat_vm,
    part_out,
    part_in,
    stat_in,
    ctx_all,
    list_sem,
    load_sem,
    ask_send,
    ask_recv,
    own_sem,
    tok_send,
    tok_recv,
    fwd_send,
    fwd_recv,
    wo_send,
    wo_recv,
    q_send,
    q_recv,
    part_send,
    part_recv,
    stat_send,
    stat_recv,
    ctx_send,
    ctx_recv,
):
    me = lax.axis_index("view")
    core = lax.axis_index("head")
    rows, width = out_ref.shape
    panel = wq_vm.shape[1]
    head_count = panel // HEAD_DIM
    depth = x_vm.shape[-1]
    block_count = x_vm.shape[0]
    plane = n // LINE
    query_blocks = rows // BLOCK
    factor = math.log2(math.e) / math.sqrt(HEAD_DIM)

    level = lax.div(me, plane)
    inner = lax.rem(level + lax.div(level, 2), 2)
    flipped = flipper(me, n)

    def half_of(step):
        return step // 2 if isinstance(step, int) else lax.div(step, 2)

    def odd(step):
        return step % 2 if isinstance(step, int) else lax.rem(step, 2)

    def reach(step):
        return LINE - 1 - step + inner * (1 - half_of(step)) * (2 * odd(step) - 1)

    def peer(offset):
        return (flipped(offset), core)

    def along(offset):
        return peer(offset * plane)

    def sibling(step):
        return lax.rem(core + step, heads)

    def before(step):
        return lax.rem(core + heads - step, heads)

    def remote(source, target, send, recv, device):
        return pltpu.make_async_remote_copy(
            src_ref=source,
            dst_ref=target,
            send_sem=send,
            recv_sem=recv,
            device_id=device,
            device_id_type=MESH,
        )

    lists = [
        pltpu.make_async_copy(source, target, list_sem.at[position])
        for position, (source, target) in enumerate(
            [(list_hbm, list_ref), (count_hbm, count_ref)]
        )
    ]
    for copy in lists:
        copy.start()
    barrier = pltpu.get_barrier_semaphore()
    for slot in range(n - 1, 0, -1):
        pl.semaphore_signal(barrier, inc=1, device_id=peer(slot), device_id_type=MESH)
    for step in range(1, heads):
        pl.semaphore_signal(
            barrier, inc=1, device_id=(me, sibling(step)), device_id_type=MESH
        )

    loads = [
        pltpu.make_async_copy(source, target, load_sem.at[position])
        for position, (source, target) in enumerate(
            [
                (x_hbm, x_vm),
                (qt_hbm, qt_vm),
                (wq_hbm, wq_vm),
                (wk_hbm, wk_vm),
                (wv_hbm, wv_vm),
                (
                    wo_hbm.at[:, pl.ds(pl.multiple_of(core * width, 128), width)],
                    wo_all.at[core],
                ),
            ]
        )
    ]
    for position in (1, 2, 0, 4, 3, 5):
        loads[position].start()

    for copy in lists:
        copy.wait()

    line_shape = (1, ask_vm.shape[1])
    first = lax.broadcasted_iota(jnp.int32, line_shape, 1) * block_count
    number = jnp.zeros(line_shape, jnp.int32)
    flags = [jnp.ones(line_shape, jnp.int32) for _ in range(query_blocks)]
    for block in range(query_blocks):
        count = count_ref[block]
        for entry in range(list_ref.shape[1]):
            distance = list_ref[block, entry] - first
            hit = jnp.logical_and(distance >= 0, distance < block_count)
            unseen = jnp.where(entry < count, 0, 1)
            number = jnp.where(hit, distance, number)
            flags[block] = jnp.minimum(flags[block], jnp.where(hit, unseen, 1))
    ask_vm[0:1] = number
    for block in range(query_blocks):
        ask_vm[block + 1 : block + 2] = flags[block]

    def ask(slot):
        return remote(
            ask_vm, asked_vm.at[slot], ask_send.at[slot], ask_recv.at[slot], peer(slot)
        )

    pl.semaphore_wait(barrier, n - 1 + heads - 1)
    for slot in range(n - 1, 0, -1):
        ask(slot).start()

    def token(step, place):
        return remote(
            picked.at[step, place],
            arrived.at[step, place, core],
            tok_send.at[step, place],
            tok_recv.at[step, place],
            peer(place),
        )

    def forward(step, place, hop, part):
        return remote(
            arrived.at[step, place, part],
            arrived.at[step, place, part],
            fwd_send.at[step, place, hop],
            fwd_recv.at[step, place, hop],
            (me, sibling(hop)),
        )

    def weight(hop, part, columns):
        return remote(
            wo_hbm.at[:, pl.ds(pl.multiple_of(columns * width, 128), width)],
            wo_all.at[part],
            wo_send.at[hop],
            wo_recv.at[hop],
            (me, sibling(hop)),
        )

    def context(hop, head, part):
        lanes = pl.ds(head * HEAD_DIM, HEAD_DIM)
        return remote(
            ctx_all.at[part, :, lanes],
            ctx_all.at[part, :, lanes],
            ctx_send.at[hop, head],
            ctx_recv.at[hop, head],
            (me, sibling(hop)),
        )

    routes = [(0, 1, 1), (0, 3, 3), (1, 3, 2), (2, 1, 3), (3, 1, 2)]

    def query(route, head):
        here, to, there = routes[route]
        return remote(
            q_vm.at[here, head],
            q_vm.at[there, head],
            q_send.at[route, head],
            q_recv.at[there, head],
            along(to),
        )

    def query_arrived(slot, head):
        return remote(
            q_vm.at[0, head],
            q_vm.at[slot, head],
            q_send.at[0, head],
            q_recv.at[slot, head],
            along(1),
        )

    def partial(step, slot, to, head):
        lanes = pl.ds(head * HEAD_DIM, HEAD_DIM)
        return remote(
            part_out.at[step, lanes],
            part_in.at[slot, lanes],
            part_send.at[step, head],
            part_recv.at[slot, head],
            along(to),
        )

    def stats(step, slot, to, head):
        return remote(
            stat_vm.at[step, head],
            stat_in.at[slot, head],
            stat_send.at[step, head],
            stat_recv.at[slot, head],
            along(to),
        )

    def merge(step, slot, head, to=None, there=None):
        lanes = pl.ds(head * HEAD_DIM, HEAD_DIM)
        stats(0, slot, 1, head).wait_recv()
        partial(0, slot, 1, head).wait_recv()
        peak, other = stat_vm[step, head, 0:1], stat_in[slot, head, 0:1]
        top = jnp.maximum(peak, other)
        mine = jnp.exp2(peak - top)
        theirs = jnp.exp2(other - top)
        stat_vm[step, head, 0:1] = top
        stat_vm[step, head, 1:2] = (
            stat_vm[step, head, 1:2] * mine + stat_in[slot, head, 1:2] * theirs
        )
        both = acc_vm[step, lanes] * mine + (
            part_in[slot, lanes].astype(jnp.float32) * theirs
        )
        if to is None:
            acc_vm[step, lanes] = both
        else:
            part_out[step, lanes] = both.astype(part_out.dtype)
            stats(step, there, to, head).start()
            partial(step, there, to, head).start()

    loads[1].wait()
    loads[2].wait()
    for head in range(head_count):
        lanes = pl.ds(head * HEAD_DIM, HEAD_DIM)
        q_vm[0, head] = jnp.dot(
            qt_vm[...], wq_vm[:, lanes], preferred_element_type=jnp.float32
        ).astype(q_vm.dtype)
        query(0, head).start()

    early = head_count - head_count // 2

    @pl.when(inner == 1)
    def _():
        for head in range(early):
            query(1, head).start()

    loads[0].wait()
    for slot in range(1, n):
        ask(slot).wait_recv()
    asked_vm[0] = ask_vm[...]
    fetch = pltpu.make_async_copy(asked_vm, asked_sm, own_sem.at[0])
    fetch.start()

    def asked(step, place, row, source):
        return asked_sm[reach(step) * plane + place, row, source]

    lane = lax.broadcasted_iota(jnp.int32, (1, ask_vm.shape[1]), 1)

    def wanted(step, place):
        row = asked_vm[reach(step) * plane + place, 0:1]
        return jnp.max(jnp.where(lane == me, row, 0))

    blocks = [[wanted(step, place) for place in range(plane)] for step in range(LINE)]
    for step in range(LINE):
        for place in range(1, plane):
            picked[step, place] = x_vm[blocks[step][place], core]
            token(step, place).start()
    @pl.when(inner == 1)
    def _():
        for head in range(head_count):
            query_arrived(1, head).wait_recv()
            query(2, head).start()
        for head in range(early, head_count):
            query(1, head).start()

    for hop in range(1, heads):
        weight(hop, core, sibling(hop)).start()
    for step in range(LINE):
        arrived[step, 0] = x_vm[blocks[step][0]]
    fetch.wait()
    loads[4].wait()
    wvt_vm[...] = wv_vm[...].T
    loads[3].wait()

    late = plane // 2
    sooner, later = range(late), range(late, plane)

    def hand_over(step, places):
        for place in places:
            if place:
                token(step, place).wait_recv()
                for hop in range(1, heads):
                    forward(step, place, hop, core).start()

    def settle(step, places):
        for place in places:
            if place:
                for hop in range(1, heads):
                    forward(step, place, hop, before(hop)).wait_recv()

    def project(step, places):
        start, size = places[0], len(places)
        tokens = arrived[step, pl.ds(start, size)].reshape(size * BLOCK, depth)
        span = pl.ds(start * BLOCK, size * BLOCK)
        k_vm[span] = jnp.dot(
            tokens, wk_vm[...], preferred_element_type=jnp.float32
        ).astype(k_vm.dtype)
        vt_vm[:, span] = lax.dot_general(
            wvt_vm[...], tokens, NT, preferred_element_type=jnp.float32
        ).astype(vt_vm.dtype)

    def give(step, head):
        lanes = pl.ds(head * HEAD_DIM, HEAD_DIM)
        part_out[step, lanes] = acc_vm[step, lanes].astype(part_out.dtype)
        stats(step, step, 1, head).start()
        partial(step, step, 1, head).start()

    def attend(step, following=None):
        lane_block = lax.broadcasted_iota(jnp.int32, (1, rows), 1) // BLOCK
        masks = []
        for place in range(plane):
            unseen = jnp.zeros((1, rows), jnp.int32)
            for block in range(query_blocks):
                flag = asked(step, 0, block + 1, flipped(place))
                unseen = jnp.where(lane_block == block, flag, unseen)
            masks.append(unseen.astype(jnp.float32) * HIDDEN)
        for head in range(head_count):
            if following is not None and head == head_count // 2:
                hand_over(following, sooner)
            lanes = pl.ds(head * HEAD_DIM, HEAD_DIM)
            scores = lax.dot_general(
                k_vm[:, lanes],
                q_vm[reach(step), head],
                NT,
                preferred_element_type=jnp.float32,
            )
            scores = [
                scores[place * BLOCK : (place + 1) * BLOCK] + masks[place]
                for place in range(plane)
            ]
            peak = functools.reduce(jnp.maximum, scores)
            peak = jnp.max(peak, axis=0, keepdims=True) * factor
            raised = [jnp.exp2(part * factor - peak) for part in scores]
            total = functools.reduce(jnp.add, raised)
            stat_vm[step, head, 0:1] = peak
            stat_vm[step, head, 1:2] = jnp.sum(total, axis=0, keepdims=True)
            probs = jnp.concatenate([part.astype(vt_vm.dtype) for part in raised], axis=0)
            acc_vm[step, lanes] = jnp.dot(
                vt_vm[lanes], probs, preferred_element_type=jnp.float32
            )

    def collect(step):
        settle(step, sooner)
        project(step, sooner)
        hand_over(step, later)
        settle(step, later)
        project(step, later)

    def tokens_sent(step):
        for place in range(1, plane):
            token(step, place).wait_send()
            for hop in range(1, heads):
                forward(step, place, hop, core).wait_send()

    def far_step(step, carry):
        collect(step)

        @pl.when(jnp.logical_and(inner == 1, step == 0))
        def _():
            for head in range(early, head_count):
                query_arrived(3, head).wait_recv()
                query(4, head).start()

        @pl.when(inner == 0)
        def _():
            for head in range(head_count):
                query_arrived(LINE - 1 - step, head).wait_recv()

        attend(step, step + 1)

        @pl.when(inner == 0)
        def _():
            for head in range(head_count):
                give(step, head)

        return carry

    def pass_back(heads_now):
        for head in heads_now:
            query_arrived(2, head).wait_recv()
            query(3, head).start()

    @pl.when(inner == 1)
    def _():
        pass_back(range(early))

    hand_over(0, sooner)

    @pl.when(inner == 1)
    def _():
        pass_back(range(early, head_count))
        for head in range(early):
            query_arrived(3, head).wait_recv()
            query(4, head).start()

    lax.fori_loop(0, LINE - 2, far_step, 0)
    near, last = LINE - 2, LINE - 1

    @pl.when(inner == 1)
    def _():
        for head in range(head_count):
            merge(0, 0, head, 3, 3)

    for slot in range(1, n):
        ask(slot).wait_send()
    for step in range(near):
        tokens_sent(step)
    for head in range(head_count):
        query(0, head).wait_send()
    collect(near)

    @pl.when(inner == 0)
    def _():
        for head in range(head_count):
            query_arrived(1, head).wait_recv()

    attend(near, last)

    @pl.when(inner == 0)
    def _():
        for head in range(head_count):
            give(near, head)

    @pl.when(inner == 1)
    def _():
        for head in range(head_count):
            merge(near, 3, head, 1, 2)
            merge(1, 1, head, 3, 4)
        for route in range(1, len(routes)):
            for head in range(head_count):
                query(route, head).wait_send()

    tokens_sent(near)
    for hop in range(1, heads):
        weight(hop, core, sibling(hop)).wait_send()
        weight(hop, before(hop), core).wait_recv()
    loads[5].wait()
    collect(last)
    attend(last)

    @pl.when(inner == 1)
    def _():
        for head in range(head_count):
            merge(last, 4, head)

    for head in range(head_count):
        lanes = pl.ds(head * HEAD_DIM, HEAD_DIM)
        merge(last, 2, head)
        merged = acc_vm[last, lanes] / stat_vm[last, head, 1:2]
        ctx_all[core, :, lanes] = merged.T.astype(ctx_all.dtype)
        for hop in range(1, heads):
            context(hop, head, core).start()
    result = jnp.dot(ctx_all[core], wo_all[core], preferred_element_type=jnp.float32)
    for hop in range(1, heads):
        part = before(hop)
        for head in range(head_count):
            context(hop, head, part).wait_recv()
        result = result + jnp.dot(
            ctx_all[part], wo_all[part], preferred_element_type=jnp.float32
        )
    out_ref[...] = result.astype(out_ref.dtype)

    tokens_sent(last)
    for step in range(LINE - 1):
        for head in range(head_count):
            stats(step, 0, 1, head).wait_send()
            partial(step, 0, 1, head).wait_send()
    for hop in range(1, heads):
        for head in range(head_count):
            context(hop, head, core).wait_send()


def per_device(query_tokens, image_tokens, w_query, w_key, w_value, w_out, vis_list, vis_count):
    n = lax.axis_size("view")
    heads = lax.axis_size("head")
    rows, depth = query_tokens.shape
    panel = w_query.shape[1]
    head_count = panel // HEAD_DIM
    width = w_out.shape[1] // heads
    block_count = image_tokens.shape[0] // BLOCK
    part_rows = BLOCK // heads
    query_blocks = vis_list.shape[0]
    plane = n // LINE
    lanes = -(-n // 128) * 128

    anywhere = pl.BlockSpec(memory_space=pltpu.HBM)
    vmem = pl.BlockSpec(memory_space=pltpu.VMEM)
    dtype = image_tokens.dtype
    dma = pltpu.SemaphoreType.DMA
    return pl.pallas_call(
        functools.partial(kernel, n, heads),
        out_shape=jax.ShapeDtypeStruct((rows, width), dtype),
        in_specs=[anywhere] * 8,
        out_specs=vmem,
        scratch_shapes=[
            pltpu.SMEM(vis_list.shape, jnp.int32),
            pltpu.SMEM(vis_count.shape, jnp.int32),
            pltpu.VMEM((block_count, heads, part_rows, depth), dtype),
            pltpu.VMEM((rows, depth), dtype),
            pltpu.VMEM((depth, panel), dtype),
            pltpu.VMEM((depth, panel), dtype),
            pltpu.VMEM((depth, panel), dtype),
            pltpu.VMEM((panel, depth), dtype),
            pltpu.VMEM((heads, panel, width), dtype),
            pltpu.VMEM((1 + query_blocks, lanes), jnp.int32),
            pltpu.VMEM((n, 1 + query_blocks, lanes), jnp.int32),
            pltpu.SMEM((n, 1 + query_blocks, lanes), jnp.int32),
            pltpu.VMEM((LINE, plane, part_rows, depth), dtype),
            pltpu.VMEM((LINE, plane, heads, part_rows, depth), dtype),
            pltpu.VMEM((LINE, head_count, rows, HEAD_DIM), dtype),
            pltpu.VMEM((plane * BLOCK, panel), dtype),
            pltpu.VMEM((panel, plane * BLOCK), dtype),
            pltpu.VMEM((LINE, panel, rows), jnp.float32),
            pltpu.VMEM((LINE, head_count, 2, rows), jnp.float32),
            pltpu.VMEM((LINE - 1, panel, rows), dtype),
            pltpu.VMEM((5, panel, rows), dtype),
            pltpu.VMEM((5, head_count, 2, rows), jnp.float32),
            pltpu.VMEM((heads, rows, panel), dtype),
            dma((2,)),
            dma((6,)),
            dma((n,)),
            dma((n,)),
            dma((1,)),
            dma((LINE, plane)),
            dma((LINE, plane)),
            dma((LINE, plane, heads)),
            dma((LINE, plane, heads)),
            dma((heads,)),
            dma((heads,)),
            dma((5, head_count)),
            dma((LINE, head_count)),
            dma((LINE - 1, head_count)),
            dma((5, head_count)),
            dma((LINE - 1, head_count)),
            dma((5, head_count)),
            dma((heads, head_count)),
            dma((heads, head_count)),
        ],
        compiler_params=pltpu.CompilerParams(
            collective_id=0, has_side_effects=True, vmem_limit_bytes=int(53.6 * 2**20)
        ),
    )(
        vis_list,
        vis_count,
        image_tokens.reshape(block_count, heads, part_rows, depth),
        query_tokens,
        w_query,
        w_key,
        w_value,
        w_out,
    )


def solution(mesh):
    return jax.shard_map(
        per_device,
        mesh=mesh,
        in_specs=(
            P("view", None),
            P("view", None),
            P(None, "head"),
            P(None, "head"),
            P(None, "head"),
            P("head", None),
            P("view", None),
            P("view"),
        ),
        out_specs=P("view", "head"),
        check_vma=False,
    )
```

```python
import functools
import math

import jax
import jax.numpy as jnp
from jax import lax
from jax.experimental import pallas as pl
from jax.experimental.pallas import tpu as pltpu
from jax.sharding import PartitionSpec as P

HEAD_DIM = 128
BLOCK = 128
LINE = 4
MESH = pl.DeviceIdType.MESH
HIDDEN = -1e30
NT = (((1,), (1,)), ((), ()))


def flipper(index, count):
    changes, bit = [], 1
    while bit < count:
        changes.append((bit, bit - 2 * bit * lax.rem(lax.div(index, bit), 2)))
        bit *= 2

    def flipped(offset):
        result = index
        for bit, change in changes:
            if offset // bit % 2:
                result = result + change
        return result

    return flipped


def kernel(
    n,
    heads,
    list_hbm,
    count_hbm,
    x_hbm,
    qt_hbm,
    wq_hbm,
    wk_hbm,
    wv_hbm,
    wo_hbm,
    out_ref,
    list_ref,
    count_ref,
    x_vm,
    qt_vm,
    wq_vm,
    wk_vm,
    wv_vm,
    wvt_vm,
    wo_all,
    ask_vm,
    asked_vm,
    asked_sm,
    picked,
    arrived,
    q_vm,
    k_vm,
    vt_vm,
    acc_vm,
    stat_vm,
    part_out,
    part_in,
    stat_in,
    ctx_all,
    list_sem,
    load_sem,
    ask_send,
    ask_recv,
    own_sem,
    tok_send,
    tok_recv,
    fwd_send,
    fwd_recv,
    wo_send,
    wo_recv,
    q_send,
    q_recv,
    part_send,
    part_recv,
    stat_send,
    stat_recv,
    ctx_send,
    ctx_recv,
):
    me = lax.axis_index("view")
    core = lax.axis_index("head")
    rows, width = out_ref.shape
    panel = wq_vm.shape[1]
    head_count = panel // HEAD_DIM
    depth = x_vm.shape[-1]
    block_count = x_vm.shape[0]
    plane = n // LINE
    query_blocks = rows // BLOCK
    factor = math.log2(math.e) / math.sqrt(HEAD_DIM)

    level = lax.div(me, plane)
    inner = lax.rem(level + lax.div(level, 2), 2)
    flipped = flipper(me, n)

    def half_of(step):
        return step // 2 if isinstance(step, int) else lax.div(step, 2)

    def odd(step):
        return step % 2 if isinstance(step, int) else lax.rem(step, 2)

    def reach(step):
        return LINE - 1 - step + inner * (1 - half_of(step)) * (2 * odd(step) - 1)

    def peer(offset):
        return (flipped(offset), core)

    def along(offset):
        return peer(offset * plane)

    def sibling(step):
        return lax.rem(core + step, heads)

    def before(step):
        return lax.rem(core + heads - step, heads)

    def remote(source, target, send, recv, device):
        return pltpu.make_async_remote_copy(
            src_ref=source,
            dst_ref=target,
            send_sem=send,
            recv_sem=recv,
            device_id=device,
            device_id_type=MESH,
        )

    lists = [
        pltpu.make_async_copy(source, target, list_sem.at[position])
        for position, (source, target) in enumerate(
            [(list_hbm, list_ref), (count_hbm, count_ref)]
        )
    ]
    for copy in lists:
        copy.start()
    barrier = pltpu.get_barrier_semaphore()
    for slot in range(n - 1, 0, -1):
        pl.semaphore_signal(barrier, inc=1, device_id=peer(slot), device_id_type=MESH)
    for step in range(1, heads):
        pl.semaphore_signal(
            barrier, inc=1, device_id=(me, sibling(step)), device_id_type=MESH
        )

    loads = [
        pltpu.make_async_copy(source, target, load_sem.at[position])
        for position, (source, target) in enumerate(
            [
                (x_hbm, x_vm),
                (qt_hbm, qt_vm),
                (wq_hbm, wq_vm),
                (wk_hbm, wk_vm),
                (wv_hbm, wv_vm),
                (
                    wo_hbm.at[:, pl.ds(pl.multiple_of(core * width, 128), width)],
                    wo_all.at[core],
                ),
            ]
        )
    ]
    for position in (1, 2, 0, 4, 3, 5):
        loads[position].start()

    for copy in lists:
        copy.wait()

    line_shape = (1, ask_vm.shape[1])
    first = lax.broadcasted_iota(jnp.int32, line_shape, 1) * block_count
    number = jnp.zeros(line_shape, jnp.int32)
    flags = [jnp.ones(line_shape, jnp.int32) for _ in range(query_blocks)]
    for block in range(query_blocks):
        count = count_ref[block]
        for entry in range(list_ref.shape[1]):
            distance = list_ref[block, entry] - first
            hit = jnp.logical_and(distance >= 0, distance < block_count)
            unseen = jnp.where(entry < count, 0, 1)
            number = jnp.where(hit, distance, number)
            flags[block] = jnp.minimum(flags[block], jnp.where(hit, unseen, 1))
    ask_vm[0:1] = number
    for block in range(query_blocks):
        ask_vm[block + 1 : block + 2] = flags[block]

    def ask(slot):
        return remote(
            ask_vm, asked_vm.at[slot], ask_send.at[slot], ask_recv.at[slot], peer(slot)
        )

    pl.semaphore_wait(barrier, n - 1 + heads - 1)
    for slot in range(n - 1, 0, -1):
        ask(slot).start()

    def token(step, place):
        return remote(
            picked.at[step, place],
            arrived.at[step, place, core],
            tok_send.at[step, place],
            tok_recv.at[step, place],
            peer(place),
        )

    def forward(step, place, hop, part):
        return remote(
            arrived.at[step, place, part],
            arrived.at[step, place, part],
            fwd_send.at[step, place, hop],
            fwd_recv.at[step, place, hop],
            (me, sibling(hop)),
        )

    def weight(hop, part, columns):
        return remote(
            wo_hbm.at[:, pl.ds(pl.multiple_of(columns * width, 128), width)],
            wo_all.at[part],
            wo_send.at[hop],
            wo_recv.at[hop],
            (me, sibling(hop)),
        )

    def context(hop, head, part):
        lanes = pl.ds(head * HEAD_DIM, HEAD_DIM)
        return remote(
            ctx_all.at[part, :, lanes],
            ctx_all.at[part, :, lanes],
            ctx_send.at[hop, head],
            ctx_recv.at[hop, head],
            (me, sibling(hop)),
        )

    routes = [(0, 1, 1), (0, 3, 3), (1, 3, 2), (2, 1, 3), (3, 1, 2)]

    def query(route, head):
        here, to, there = routes[route]
        return remote(
            q_vm.at[here, head],
            q_vm.at[there, head],
            q_send.at[route, head],
            q_recv.at[there, head],
            along(to),
        )

    def query_arrived(slot, head):
        return remote(
            q_vm.at[0, head],
            q_vm.at[slot, head],
            q_send.at[0, head],
            q_recv.at[slot, head],
            along(1),
        )

    def partial(step, slot, to, head):
        lanes = pl.ds(head * HEAD_DIM, HEAD_DIM)
        return remote(
            part_out.at[step, lanes],
            part_in.at[slot, lanes],
            part_send.at[step, head],
            part_recv.at[slot, head],
            along(to),
        )

    def stats(step, slot, to, head):
        return remote(
            stat_vm.at[step, head],
            stat_in.at[slot, head],
            stat_send.at[step, head],
            stat_recv.at[slot, head],
            along(to),
        )

    def merge(step, slot, head, to=None, there=None):
        lanes = pl.ds(head * HEAD_DIM, HEAD_DIM)
        stats(0, slot, 1, head).wait_recv()
        partial(0, slot, 1, head).wait_recv()
        peak, other = stat_vm[step, head, 0:1], stat_in[slot, head, 0:1]
        top = jnp.maximum(peak, other)
        mine = jnp.exp2(peak - top)
        theirs = jnp.exp2(other - top)
        stat_vm[step, head, 0:1] = top
        stat_vm[step, head, 1:2] = (
            stat_vm[step, head, 1:2] * mine + stat_in[slot, head, 1:2] * theirs
        )
        both = acc_vm[step, lanes] * mine + (
            part_in[slot, lanes].astype(jnp.float32) * theirs
        )
        if to is None:
            acc_vm[step, lanes] = both
        else:
            part_out[step, lanes] = both.astype(part_out.dtype)
            stats(step, there, to, head).start()
            partial(step, there, to, head).start()

    loads[1].wait()
    loads[2].wait()
    for head in range(head_count):
        lanes = pl.ds(head * HEAD_DIM, HEAD_DIM)
        q_vm[0, head] = jnp.dot(
            qt_vm[...], wq_vm[:, lanes], preferred_element_type=jnp.float32
        ).astype(q_vm.dtype)

    early = head_count - head_count // 2
    most = head_count - head_count // 4
    for head in range(most):
        query(0, head).start()

    @pl.when(inner == 0)
    def _():
        for head in range(most, head_count):
            query(0, head).start()

    @pl.when(inner == 1)
    def _():
        for head in range(early):
            query(1, head).start()

    loads[0].wait()
    for slot in range(1, n):
        ask(slot).wait_recv()
    asked_vm[0] = ask_vm[...]
    fetch = pltpu.make_async_copy(asked_vm, asked_sm, own_sem.at[0])
    fetch.start()

    def asked(step, place, row, source):
        return asked_sm[reach(step) * plane + place, row, source]

    lane = lax.broadcasted_iota(jnp.int32, (1, ask_vm.shape[1]), 1)

    def wanted(step, place):
        row = asked_vm[reach(step) * plane + place, 0:1]
        return jnp.max(jnp.where(lane == me, row, 0))

    blocks = [[wanted(step, place) for place in range(plane)] for step in range(LINE)]
    for step in range(LINE):
        for place in range(1, plane):
            picked[step, place] = x_vm[blocks[step][place], core]
            token(step, place).start()
    @pl.when(inner == 1)
    def _():
        for head in range(head_count):
            query_arrived(1, head).wait_recv()
            query(2, head).start()
        for head in range(early, head_count):
            query(1, head).start()

    for hop in range(1, heads):
        weight(hop, core, sibling(hop)).start()
    for step in range(LINE):
        arrived[step, 0] = x_vm[blocks[step][0]]
    fetch.wait()
    loads[4].wait()
    wvt_vm[...] = wv_vm[...].T
    loads[3].wait()

    late = plane // 2
    sooner, later = range(late), range(late, plane)

    def hand_over(step, places):
        for place in places:
            if place:
                token(step, place).wait_recv()
                for hop in range(1, heads):
                    forward(step, place, hop, core).start()

    def settle(step, places):
        for place in places:
            if place:
                for hop in range(1, heads):
                    forward(step, place, hop, before(hop)).wait_recv()

    def project(step, places):
        start, size = places[0], len(places)
        tokens = arrived[step, pl.ds(start, size)].reshape(size * BLOCK, depth)
        span = pl.ds(start * BLOCK, size * BLOCK)
        k_vm[span] = jnp.dot(
            tokens, wk_vm[...], preferred_element_type=jnp.float32
        ).astype(k_vm.dtype)
        vt_vm[:, span] = lax.dot_general(
            wvt_vm[...], tokens, NT, preferred_element_type=jnp.float32
        ).astype(vt_vm.dtype)

    def give(step, head):
        lanes = pl.ds(head * HEAD_DIM, HEAD_DIM)
        part_out[step, lanes] = acc_vm[step, lanes].astype(part_out.dtype)
        stats(step, step, 1, head).start()
        partial(step, step, 1, head).start()

    def attend(step, following=None):
        lane_block = lax.broadcasted_iota(jnp.int32, (1, rows), 1) // BLOCK
        masks = []
        for place in range(plane):
            unseen = jnp.zeros((1, rows), jnp.int32)
            for block in range(query_blocks):
                flag = asked(step, 0, block + 1, flipped(place))
                unseen = jnp.where(lane_block == block, flag, unseen)
            masks.append(unseen.astype(jnp.float32) * HIDDEN)
        for head in range(head_count):
            if following is not None and head == head_count // 2:
                hand_over(following, sooner)
            lanes = pl.ds(head * HEAD_DIM, HEAD_DIM)
            scores = lax.dot_general(
                k_vm[:, lanes],
                q_vm[reach(step), head],
                NT,
                preferred_element_type=jnp.float32,
            )
            scores = [
                scores[place * BLOCK : (place + 1) * BLOCK] + masks[place]
                for place in range(plane)
            ]
            peak = functools.reduce(jnp.maximum, scores)
            peak = jnp.max(peak, axis=0, keepdims=True) * factor
            raised = [jnp.exp2(part * factor - peak) for part in scores]
            total = functools.reduce(jnp.add, raised)
            stat_vm[step, head, 0:1] = peak
            stat_vm[step, head, 1:2] = jnp.sum(total, axis=0, keepdims=True)
            probs = jnp.concatenate([part.astype(vt_vm.dtype) for part in raised], axis=0)
            acc_vm[step, lanes] = jnp.dot(
                vt_vm[lanes], probs, preferred_element_type=jnp.float32
            )

    def collect(step):
        settle(step, sooner)
        project(step, sooner)
        hand_over(step, later)
        settle(step, later)
        project(step, later)

    def tokens_sent(step):
        for place in range(1, plane):
            token(step, place).wait_send()
            for hop in range(1, heads):
                forward(step, place, hop, core).wait_send()

    def far_step(step, carry):
        collect(step)

        @pl.when(jnp.logical_and(inner == 1, step == 0))
        def _():
            for head in range(early, head_count):
                query_arrived(3, head).wait_recv()
                query(4, head).start()

        @pl.when(jnp.logical_and(inner == 1, step == 0))
        def _():
            for head in range(most, head_count):
                query(0, head).start()

        @pl.when(inner == 0)
        def _():
            for head in range(head_count):
                query_arrived(LINE - 1 - step, head).wait_recv()

        attend(step, step + 1)

        @pl.when(inner == 0)
        def _():
            for head in range(head_count):
                give(step, head)

        return carry

    def pass_back(heads_now):
        for head in heads_now:
            query_arrived(2, head).wait_recv()
            query(3, head).start()

    @pl.when(inner == 1)
    def _():
        pass_back(range(early))

    hand_over(0, sooner)

    @pl.when(inner == 1)
    def _():
        pass_back(range(early, head_count))
        for head in range(early):
            query_arrived(3, head).wait_recv()
            query(4, head).start()

    lax.fori_loop(0, LINE - 2, far_step, 0)
    near, last = LINE - 2, LINE - 1

    @pl.when(inner == 1)
    def _():
        for head in range(head_count):
            merge(0, 0, head, 3, 3)

    for slot in range(1, n):
        ask(slot).wait_send()
    for step in range(near):
        tokens_sent(step)
    for head in range(head_count):
        query(0, head).wait_send()
    collect(near)

    @pl.when(inner == 0)
    def _():
        for head in range(head_count):
            query_arrived(1, head).wait_recv()

    attend(near, last)

    @pl.when(inner == 0)
    def _():
        for head in range(head_count):
            give(near, head)

    @pl.when(inner == 1)
    def _():
        for head in range(head_count):
            merge(near, 3, head, 1, 2)
            merge(1, 1, head, 3, 4)
        for route in range(1, len(routes)):
            for head in range(head_count):
                query(route, head).wait_send()

    tokens_sent(near)
    for hop in range(1, heads):
        weight(hop, core, sibling(hop)).wait_send()
        weight(hop, before(hop), core).wait_recv()
    loads[5].wait()
    collect(last)
    attend(last)

    @pl.when(inner == 1)
    def _():
        for head in range(head_count):
            merge(last, 4, head)

    for head in range(head_count):
        lanes = pl.ds(head * HEAD_DIM, HEAD_DIM)
        merge(last, 2, head)
        merged = acc_vm[last, lanes] / stat_vm[last, head, 1:2]
        ctx_all[core, :, lanes] = merged.T.astype(ctx_all.dtype)
        for hop in range(1, heads):
            context(hop, head, core).start()
    result = jnp.dot(ctx_all[core], wo_all[core], preferred_element_type=jnp.float32)
    for hop in range(1, heads):
        part = before(hop)
        for head in range(head_count):
            context(hop, head, part).wait_recv()
        result = result + jnp.dot(
            ctx_all[part], wo_all[part], preferred_element_type=jnp.float32
        )
    out_ref[...] = result.astype(out_ref.dtype)

    tokens_sent(last)
    for step in range(LINE - 1):
        for head in range(head_count):
            stats(step, 0, 1, head).wait_send()
            partial(step, 0, 1, head).wait_send()
    for hop in range(1, heads):
        for head in range(head_count):
            context(hop, head, core).wait_send()


def per_device(query_tokens, image_tokens, w_query, w_key, w_value, w_out, vis_list, vis_count):
    n = lax.axis_size("view")
    heads = lax.axis_size("head")
    rows, depth = query_tokens.shape
    panel = w_query.shape[1]
    head_count = panel // HEAD_DIM
    width = w_out.shape[1] // heads
    block_count = image_tokens.shape[0] // BLOCK
    part_rows = BLOCK // heads
    query_blocks = vis_list.shape[0]
    plane = n // LINE
    lanes = -(-n // 128) * 128

    anywhere = pl.BlockSpec(memory_space=pltpu.HBM)
    vmem = pl.BlockSpec(memory_space=pltpu.VMEM)
    dtype = image_tokens.dtype
    dma = pltpu.SemaphoreType.DMA
    return pl.pallas_call(
        functools.partial(kernel, n, heads),
        out_shape=jax.ShapeDtypeStruct((rows, width), dtype),
        in_specs=[anywhere] * 8,
        out_specs=vmem,
        scratch_shapes=[
            pltpu.SMEM(vis_list.shape, jnp.int32),
            pltpu.SMEM(vis_count.shape, jnp.int32),
            pltpu.VMEM((block_count, heads, part_rows, depth), dtype),
            pltpu.VMEM((rows, depth), dtype),
            pltpu.VMEM((depth, panel), dtype),
            pltpu.VMEM((depth, panel), dtype),
            pltpu.VMEM((depth, panel), dtype),
            pltpu.VMEM((panel, depth), dtype),
            pltpu.VMEM((heads, panel, width), dtype),
            pltpu.VMEM((1 + query_blocks, lanes), jnp.int32),
            pltpu.VMEM((n, 1 + query_blocks, lanes), jnp.int32),
            pltpu.SMEM((n, 1 + query_blocks, lanes), jnp.int32),
            pltpu.VMEM((LINE, plane, part_rows, depth), dtype),
            pltpu.VMEM((LINE, plane, heads, part_rows, depth), dtype),
            pltpu.VMEM((LINE, head_count, rows, HEAD_DIM), dtype),
            pltpu.VMEM((plane * BLOCK, panel), dtype),
            pltpu.VMEM((panel, plane * BLOCK), dtype),
            pltpu.VMEM((LINE, panel, rows), jnp.float32),
            pltpu.VMEM((LINE, head_count, 2, rows), jnp.float32),
            pltpu.VMEM((LINE - 1, panel, rows), dtype),
            pltpu.VMEM((5, panel, rows), dtype),
            pltpu.VMEM((5, head_count, 2, rows), jnp.float32),
            pltpu.VMEM((heads, rows, panel), dtype),
            dma((2,)),
            dma((6,)),
            dma((n,)),
            dma((n,)),
            dma((1,)),
            dma((LINE, plane)),
            dma((LINE, plane)),
            dma((LINE, plane, heads)),
            dma((LINE, plane, heads)),
            dma((heads,)),
            dma((heads,)),
            dma((5, head_count)),
            dma((LINE, head_count)),
            dma((LINE - 1, head_count)),
            dma((5, head_count)),
            dma((LINE - 1, head_count)),
            dma((5, head_count)),
            dma((heads, head_count)),
            dma((heads, head_count)),
        ],
        compiler_params=pltpu.CompilerParams(
            collective_id=0, has_side_effects=True, vmem_limit_bytes=int(53.6 * 2**20)
        ),
    )(
        vis_list,
        vis_count,
        image_tokens.reshape(block_count, heads, part_rows, depth),
        query_tokens,
        w_query,
        w_key,
        w_value,
        w_out,
    )


def solution(mesh):
    return jax.shard_map(
        per_device,
        mesh=mesh,
        in_specs=(
            P("view", None),
            P("view", None),
            P(None, "head"),
            P(None, "head"),
            P(None, "head"),
            P("head", None),
            P("view", None),
            P("view"),
        ),
        out_specs=P("view", "head"),
        check_vma=False,
    )
```
